512 devices in a mesh: row: 32 (over z_lo, y), col: 16 (over x, z_hi, core).
Axes of the slice: x: 4, y: 8, z: 8 (z_hi: 2, z_lo: 4; z = z_hi * 4 + z_lo), core: 2. Of those that a mesh axis runs over, the one named last changes fastest.
Arguments:
- eigvecs: float32 [8192, 2048], P('row', 'col'), may hold values from -6 to 6
- reflectors: float32 [8, 32, 256, 512], P(None, 'row', 'col'), may hold values from -1 to 1
- factors: float32 [8, 32, 256, 256], P(None, 'row', 'col'), as said below
- offsets: int32 [8, 32], P(None, 'row'), may hold values from 0 to 255
- sweep_order: int32 [8], replicated, may hold values from 0 to 7, each once
Outputs:
- rotated: float32 [8192, 2048], P('row', 'col')
The draws below stay inside these ranges and needn't reach their ends.
Inputs may be any that keep to these rules, and one draw needn't show every extreme that they name: `factors`: zero below the diagonal. `sweep_order`: each number of 0 to 7 appears once; only the first 2 entries are used.
All inputs are finite; a program needn't handle non-finite values.
Results may differ from the reference program's by a relative error of at most 0.0003.
Values sent between devices are 32-bit elements; how exact they have to be, the bound alone decides.
A program may use at most 64 MiB of HBM per device.

```python
import jax
import jax.numpy as jnp
from jax import lax

NB = 256
POOL = 8
FLIGHT = 2
BLOCKS = 32
ORDER = 8192
NCOLS = 2048


PRECISE = lax.Precision.HIGHEST


def shared_offsets(key):
    return jax.random.randint(jax.random.fold_in(key, 11), (POOL, BLOCKS), 0, NB).astype(jnp.int32)


def raw_vectors(key):
    inner_key = jax.random.fold_in(key, 23)
    full_shape = (POOL, BLOCKS, NB, 2 * NB)
    values = jnp.clip(jax.random.normal(inner_key, full_shape, jnp.float32), -4.0, 4.0)
    return values / jnp.sqrt(jnp.float32(NB))


def masked_vectors(raw_entries, start_shift):
    reflector = lax.broadcasted_iota(jnp.int32, raw_entries.shape, 2)
    position = lax.broadcasted_iota(jnp.int32, raw_entries.shape, 3)
    start_row = reflector + start_shift[:, :, None, None]
    live_mask = (position >= start_row) & (position < start_row + NB)
    kept = jnp.where(live_mask, raw_entries, jnp.zeros_like(raw_entries))
    return jnp.where(position == start_row, jnp.ones_like(raw_entries), kept)


def draw_offsets(key, part):
    return shared_offsets(key)


def draw_reflectors(key, part):
    return raw_vectors(key)


def draw_factors(key, part):
    vectors = masked_vectors(raw_vectors(key), shared_offsets(key))
    gram = jnp.einsum('pbci,pbdi->pbcd', vectors, vectors, precision=PRECISE)
    identity = jnp.eye(NB, dtype=jnp.float32)
    inverse = jnp.triu(gram, 1) + gram * identity * 0.5
    target = jnp.broadcast_to(identity, inverse.shape)
    return lax.linalg.triangular_solve(inverse, target, left_side=True, lower=False)


def block_scale(own_key, extent, pieces, least, top_value):
    factor_of, own = 1.0, jax.random.fold_in(own_key, 6)
    for axis_at, shards_of in pieces:
        steps = jnp.exp(jax.random.uniform(jax.random.fold_in(own, axis_at), (shards_of,), jnp.float32, least / len(pieces), top_value / len(pieces)))
        factor_of = factor_of * jnp.repeat(steps, extent[axis_at] // shards_of).reshape([-1 if axis == axis_at else 1 for axis in range(len(extent))])
    return factor_of


def centred(rng, shape, scale, bound, split=(), kind=jnp.bfloat16):
    entries = scale * jax.random.normal(rng, shape, jnp.float32)
    if split:
        entries = entries * block_scale(rng, shape, split, -0.22, 0.18)
    return jnp.clip(entries, -bound, bound).astype(kind)


def setup_inputs(seed: int = 0) -> dict:
    keys = jax.random.split(jax.random.key(seed), 6)
    return {
        "eigvecs": centred(keys[0], (ORDER, NCOLS), 1.0, 6.0, ((0, 32), (1, 16)), jnp.float32),
        "reflectors": draw_reflectors(jax.random.fold_in(keys[5], 71), 0),
        "factors": draw_factors(jax.random.fold_in(keys[5], 71), 0),
        "offsets": draw_offsets(jax.random.fold_in(keys[5], 71), 0),
        "sweep_order": jax.random.permutation(keys[4], POOL).astype(jnp.int32),
    }


PRECISE = lax.Precision.HIGHEST

def matmul(left_side, right_side):
    return jnp.dot(left_side.astype(jnp.float32), right_side.astype(jnp.float32), precision=PRECISE, preferred_element_type=jnp.float32)

def transposed_product(left_side, right_side):
    return lax.dot_general(left_side.astype(jnp.float32), right_side.astype(jnp.float32), (((0,), (0,)), ((), ())), precision=PRECISE, preferred_element_type=jnp.float32)

def staircase(raw_entries, start_shift, column_base):
    reflector_count, height = raw_entries.shape
    reflector = column_base + lax.broadcasted_iota(jnp.int32, (reflector_count, height), 0)
    position = lax.broadcasted_iota(jnp.int32, (reflector_count, height), 1)
    start_row = reflector + start_shift
    live_mask = (position >= start_row) & (position < start_row + height // 2)
    kept = jnp.where(live_mask, raw_entries, jnp.zeros_like(raw_entries))
    return jnp.where(position == start_row, jnp.ones_like(raw_entries), kept)

def reference(eigvecs, reflectors, factors, offsets, sweep_order):
    height = eigvecs.shape[0]
    width = eigvecs.shape[1]
    current = eigvecs
    for step in range(FLIGHT):
        chosen = sweep_order[step]
        set_vectors = reflectors[chosen]
        set_factors = factors[chosen]
        set_offsets = offsets[chosen]
        padded = jnp.concatenate([current, jnp.zeros((NB, width), eigvecs.dtype)], 0)

        def apply_block(block_index, state):
            block_index = jnp.asarray(block_index).astype(jnp.int32)
            raw_entries = lax.dynamic_index_in_dim(set_vectors, block_index, 0, keepdims=False)
            start_shift = lax.dynamic_index_in_dim(set_offsets, block_index, 0, keepdims=False)
            factor = lax.dynamic_index_in_dim(set_factors, block_index, 0, keepdims=False)
            vectors = staircase(raw_entries, start_shift, 0)
            first_row = (block_index * NB).astype(jnp.int32)
            block_rows = lax.dynamic_slice_in_dim(state, first_row, 2 * NB, 0)
            coeffs = matmul(factor, matmul(vectors, block_rows))
            block_rows = block_rows - transposed_product(vectors, coeffs)
            return lax.dynamic_update_slice_in_dim(state, block_rows, first_row, 0)
        padded = lax.fori_loop(0, BLOCKS, apply_block, padded)
        current = padded[:height]
    return current
```

```python
import functools

import jax
import jax.numpy as jnp
from jax import lax
from jax.experimental import pallas as pl
from jax.experimental.pallas import tpu as pltpu
from jax.sharding import PartitionSpec as P

MESH = pl.DeviceIdType.MESH
F32, BF16 = jnp.float32, jnp.bfloat16
NN, NT = ((1,), (0,)), ((1,), (1,))

Z_LO, Y, X, Z_HI, CORES = 4, 8, 4, 2, 2


def split(value):
    high = value.astype(BF16)
    return high, (value - high.astype(F32)).astype(BF16)


def dot(left, right, dims):
    return lax.dot_general(left, right, (dims, ((), ())), preferred_element_type=F32)


def product(left, right, dims):
    (lh, ll), (rh, rl) = left, right
    return dot(lh, rh, dims) + (dot(lh, rl, dims) + dot(ll, rh, dims))


def kernel(
    dims,
    order_ref,
    offs_ref,
    eig_ref,
    refl_ref,
    fact_ref,
    out_ref,
    vf,
    ops_h,
    ops_l,
    proj,
    below_raw,
    below,
    init,
    gains,
    gains_h,
    gains_l,
    d_out,
    d_in,
    carry_in,
    carry_out,
    states_out,
    states_in,
    z_s,
    z_r,
    x_s,
    x_r,
    q_s,
    q_r,
    e_s,
    e_r,
    g_s,
    g_r,
    gq_s,
    gq_r,
    d_s,
    d_r,
    i_s,
    c_s,
    c_r,
    s_s,
    s_r,
    f_s,
    f_r,
):
    KZ, NY, NX, NH, NQ = dims
    NB = eig_ref.shape[0]
    CL = eig_ref.shape[1]
    CW = CL // NY
    RC = refl_ref.shape[2]
    HALF = NB // NQ
    PART = HALF // 2
    FAR = NY // 2

    row, col = lax.axis_index("row"), lax.axis_index("col")
    k, y = row // NY, row % NY
    x, h, q = col // (NH * NQ), (col // NQ) % NH, col % NQ
    last_row = KZ * NY - 1

    def y_peer(d):
        return (k * NY + (y + d) % NY, col)

    def x_peer(d):
        return (row, ((x + d) % NX) * (NH * NQ) + h * NQ + q)

    z_peer = (row, x * (NH * NQ) + (1 - h) * NQ + q)
    sibling = (row, x * (NH * NQ) + h * NQ + (1 - q))
    up_group, down_group = (row - NY, col), (row + NY, col)
    up_row, down_row = (row - 1, col), (row + 1, col)

    def copy(src, dst, ssem, rsem, device):
        return pltpu.make_async_remote_copy(
            src_ref=src,
            dst_ref=dst,
            send_sem=ssem,
            recv_sem=rsem,
            device_id=device,
            device_id_type=MESH,
        )

    def arrived(dst, rsem):
        copy(dst, dst, z_s.at[0], rsem, sibling).wait_recv()

    barrier = pltpu.get_barrier_semaphore()

    def greet(device):
        pl.semaphore_signal(barrier, inc=1, device_id=device, device_id_type=MESH)

    greet(z_peer)
    greet(sibling)
    for d in range(1, NX):
        greet(x_peer(d))
    for d in range(1, NY):
        greet(y_peer(d))
    has_up, has_down = k > 0, k < KZ - 1
    first_y, final_y = y == 0, y == NY - 1

    @pl.when(has_up)
    def _():
        greet(up_group)

    @pl.when(has_down)
    def _():
        greet(down_group)

    @pl.when(has_up & first_y)
    def _():
        greet(up_row)

    @pl.when(has_down & final_y)
    def _():
        greet(down_row)

    def start_of(t):
        return offs_ref[order_ref[t], 0]

    for t in range(2):
        chosen = order_ref[t]
        raw = refl_ref[chosen, 0]
        start = (
            col * RC + start_of(t) + lax.broadcasted_iota(jnp.int32, (RC, NB), 0)
        )
        position = lax.broadcasted_iota(jnp.int32, (RC, NB), 1)
        upper, lower = raw[:, :NB], raw[:, NB:]
        packed = jnp.where(position + NB >= start, lower, jnp.zeros_like(lower))
        packed = jnp.where(position >= start, upper, packed)
        unit = (position == start) | (position + NB == start)
        vf[t, x, h, q, pl.ds(0, RC)] = jnp.where(unit, jnp.ones_like(packed), packed)
        vf[t, x, h, q, pl.ds(RC, RC)] = fact_ref[chosen, 0]

    expected = (
        2
        + (NX - 1)
        + (NY - 1)
        + has_up.astype(jnp.int32)
        + has_down.astype(jnp.int32)
        + (has_up & first_y).astype(jnp.int32)
        + (has_down & final_y).astype(jnp.int32)
    )
    pl.semaphore_wait(barrier, expected)

    def z_send(t):
        piece = vf.at[t, x, h, q]
        return copy(piece, piece, z_s.at[t], z_r.at[t], z_peer)

    def x_send(t, p, d):
        piece = vf.at[t, x, h if p == 0 else 1 - h, q]
        return copy(piece, piece, x_s.at[t, p, d], x_r.at[t, p, d], x_peer(d))

    def q_send(t, p, d):
        piece = vf.at[t, (x + NX - d) % NX, h if p == 0 else 1 - h, q]
        return copy(piece, piece, q_s.at[t, p, d], q_r.at[t, p, d], sibling)

    def x_take(t, p, d):
        piece = vf.at[t, (x + NX - d) % NX, h if p == 0 else 1 - h, q]
        arrived(piece, x_r.at[t, p, d])
        q_send(t, p, d).start()

    def q_take(t):
        for p in range(NH):
            for d in range(NX):
                piece = vf.at[t, (x + NX - d) % NX, h if p == 0 else 1 - h, 1 - q]
                arrived(piece, q_r.at[t, p, d])

    def z_take(t):
        arrived(vf.at[t, x, 1 - h, q], z_r.at[t])
        for d in range(1, NX):
            x_send(t, 1, d).start()
        q_send(t, 1, 0).start()

    def e_send():
        return copy(eig_ref, below_raw, e_s, e_r, up_row)

    near_first = sorted(range(1, NX), key=lambda d: min(d, NX - d))
    for t in range(2):
        z_send(t).start()
    for t in range(2):
        for d in near_first:
            x_send(t, 0, d).start()
        q_send(t, 0, 0).start()

    @pl.when(row > 0)
    def _():
        e_send().start()

    def init_send(t, d):
        there = pl.ds(((y + d) % NY) * CW, CW)
        return copy(
            init.at[t, there], carry_in.at[t], i_s.at[t, d], c_r.at[t], y_peer(d)
        )

    def send_init(t):
        for d in range(1, NY):
            init_send(t, d).start()
        carry_in[t] = init[t, pl.ds(0, CW)]

    @pl.when(row == 0)
    def _():
        init[0] = jnp.transpose(eig_ref[...])
        send_init(0)

    z_take(0)
    for d in near_first:
        x_take(0, 0, d)
    z_take(1)
    for d in near_first:
        x_take(0, 1, d)

    @pl.when(row < last_row)
    def _():
        arrived(below_raw, e_r)
        below[0] = jnp.transpose(below_raw[...])

    @pl.when(row == last_row)
    def _():
        below[0] = jnp.zeros((CL, NB), F32)

    q_take(0)

    UP, LOW, FAC = 0, 1, 2

    def parts(t, which):
        return ops_h[t, which], ops_l[t, which]

    def unpack(t):
        both = vf[t, :, :, :, pl.ds(0, RC), :].reshape(NB, NB)
        factor = vf[t, :, :, :, pl.ds(RC, RC), :].reshape(NB, NB)
        start = lax.broadcasted_iota(jnp.int32, (NB, NB), 0) + start_of(t)
        position = lax.broadcasted_iota(jnp.int32, (NB, NB), 1)
        zero = jnp.zeros_like(both)
        for which, value in (
            (UP, jnp.where(position >= start, both, zero)),
            (LOW, jnp.where(position < start, both, zero)),
            (FAC, factor),
        ):
            ops_h[t, which], ops_l[t, which] = split(value)

    def make_gain(t):
        inner = product(parts(t, FAC), parts(t, UP), NN)
        turned = jnp.transpose(inner)
        gains[t, y] = -product(split(turned), parts(t, LOW), NN)

    def make_shift(t):
        rows = below[t]
        lowered = product(split(rows), parts(t, LOW), NT)
        proj[t] = lowered
        coeffs = product(split(lowered), parts(t, FAC), NT)
        d_out[t] = rows - product(split(coeffs), parts(t, LOW), NN)

    def finish(t):
        rows = states_in[t]
        coeffs = product(split(rows), parts(t, UP), NT) + proj[t]
        coeffs = product(split(coeffs), parts(t, FAC), NT)
        return rows - product(split(coeffs), parts(t, UP), NN)

    def ring_ids():
        for d in range(1, FAR + 1):
            for m in range(2):
                for way in range(2):
                    if d < FAR or m == way:
                        yield way, d, m

    def part_rows(m):
        return pl.ds(pl.multiple_of(q * HALF + m * PART, PART), PART)

    def ring_send(t, way, d, m):
        source = (y + NY - (d - 1)) % NY if way == 0 else (y + (d - 1)) % NY
        piece = gains.at[t, source, part_rows(m)]
        there = y_peer(1 if way == 0 else NY - 1)
        return copy(
            piece, piece, g_s.at[t, way, d, m], g_r.at[t, way, d, m], there
        )

    def ring_source(way, d):
        return (y + NY - d) % NY if way == 0 else (y + d) % NY

    def ring_pass(t, way, d, m):
        piece = gains.at[t, ring_source(way, d), part_rows(m)]
        return copy(
            piece, piece, gq_s.at[t, way, d, m], gq_r.at[t, way, d, m], sibling
        )

    def ring_start(t):
        for way, d, m in ring_ids():
            if d == 1:
                ring_send(t, way, d, m).start()

    def ring_run(t):
        ids = list(ring_ids())
        for way, d, m in ids:
            arrived(
                gains.at[t, ring_source(way, d), part_rows(m)], g_r.at[t, way, d, m]
            )
            if (way, d + 1, m) in ids:
                ring_send(t, way, d + 1, m).start()
            ring_pass(t, way, d, m).start()
        for way, d, m in ids:
            other = pl.ds(pl.multiple_of((1 - q) * HALF + m * PART, PART), PART)
            arrived(gains.at[t, ring_source(way, d), other], gq_r.at[t, way, d, m])

        def convert(i, carry):
            gains_h[t, i], gains_l[t, i] = split(gains[t, i])
            return carry

        lax.fori_loop(0, NY, convert, 0)

    def d_send(t, d):
        there = pl.ds(((y + d) % NY) * CW, CW)
        return copy(
            d_out.at[t, there], d_in.at[t, y], d_s.at[t, d], d_r.at[t, d], y_peer(d)
        )

    def send_shift(t):
        for d in range(1, NY):
            d_send(t, d).start()
        d_in[t, y] = d_out[t, pl.ds(y * CW, CW)]

    def take_shift(t):
        for d in range(1, NY):
            arrived(d_in.at[t, (y + NY - d) % NY], d_r.at[t, d])

    def state_send(t, i):
        return copy(
            states_out.at[t, i],
            states_in.at[t, pl.ds(y * CW, CW)],
            s_s.at[t, i],
            s_r.at[t, y],
            (k * NY + i, col),
        )

    def carry_send(t):
        return copy(carry_out.at[t], carry_in.at[t], c_s.at[t], c_r.at[t], down_group)

    def chain(t):
        take_shift(t)

        @pl.when(row > 0)
        def _():
            arrived(carry_in.at[t], c_r.at[t])

        state = carry_in[t]
        for i in range(NY):
            states_out[t, i] = state

            @pl.when(y != i)
            def _():
                state_send(t, i).start()

            high, low = split(state)
            gain_h = gains_h[t, i]
            pair = dot(jnp.concatenate([high, low], 0), gain_h, NN)
            state = (pair[:CW] + pair[CW:]) + (
                dot(high, gains_l[t, i], NN) + d_in[t, i]
            )
        carry_out[t] = state

        @pl.when(has_down)
        def _():
            carry_send(t).start()

    def collect(t):
        mine = pl.ds(y * CW, CW)
        states_in[t, mine] = states_out[t, y]
        for d in range(1, NY):
            source = (y + d) % NY
            arrived(states_in.at[t, pl.ds(source * CW, CW)], s_r.at[t, source])

    def f_send():
        return copy(init.at[1], below.at[1], f_s, f_r, up_row)

    unpack(0)
    make_gain(0)
    ring_start(0)
    make_shift(0)
    send_shift(0)
    for d in near_first:
        x_take(1, 0, d)
    for d in near_first:
        x_take(1, 1, d)
    q_take(1)
    unpack(1)
    make_gain(1)
    ring_run(0)

    @pl.when(k >= KZ // 2)
    def _():
        ring_start(1)
        ring_run(1)

    chain(0)

    @pl.when(k < KZ // 2)
    def _():
        ring_start(1)
        ring_run(1)

    collect(0)
    init[1] = finish(0)

    @pl.when(row > 0)
    def _():
        f_send().start()

    @pl.when(row == 0)
    def _():
        send_init(1)

    @pl.when(row < last_row)
    def _():
        arrived(below.at[1], f_r)

    @pl.when(row == last_row)
    def _():
        below[1] = jnp.zeros((CL, NB), F32)

    make_shift(1)
    send_shift(1)
    chain(1)
    collect(1)
    out_ref[...] = jnp.transpose(finish(1))

    for t in range(2):
        z_send(t).wait_send()
        for p in range(NH):
            for d in range(NX):
                if d:
                    x_send(t, p, d).wait_send()
                q_send(t, p, d).wait_send()
        for way, d, m in ring_ids():
            ring_send(t, way, d, m).wait_send()
            ring_pass(t, way, d, m).wait_send()
        for d in range(1, NY):
            d_send(t, d).wait_send()
        for i in range(NY):

            @pl.when(y != i)
            def _():
                state_send(t, i).wait_send()

        @pl.when(has_down)
        def _():
            carry_send(t).wait_send()

        @pl.when(row == 0)
        def _():
            for d in range(1, NY):
                init_send(t, d).wait_send()

    @pl.when(row > 0)
    def _():
        e_send().wait_send()
        f_send().wait_send()


def on_device(dims, eigvecs, reflectors, factors, offsets, sweep_order):
    KZ, NY, NX, NH, NQ = dims
    NB, CL = eigvecs.shape
    CW = CL // NY
    RC = reflectors.shape[2]
    FAR = NY // 2
    DMA = pltpu.SemaphoreType.DMA
    vmem = pl.BlockSpec(memory_space=pltpu.VMEM)
    smem = pl.BlockSpec(memory_space=pltpu.SMEM)
    return pl.pallas_call(
        functools.partial(kernel, dims),
        out_shape=jax.ShapeDtypeStruct((NB, CL), F32),
        in_specs=[smem, smem, vmem, vmem, vmem],
        out_specs=vmem,
        scratch_shapes=[
            pltpu.VMEM((2, NX, NH, NQ, 2 * RC, NB), F32),
            pltpu.VMEM((2, 3, NB, NB), BF16),
            pltpu.VMEM((2, 3, NB, NB), BF16),
            pltpu.VMEM((2, CL, NB), F32),
            pltpu.VMEM((NB, CL), F32),
            pltpu.VMEM((2, CL, NB), F32),
            pltpu.VMEM((2, CL, NB), F32),
            pltpu.VMEM((2, NY, NB, NB), F32),
            pltpu.VMEM((2, NY, NB, NB), BF16),
            pltpu.VMEM((2, NY, NB, NB), BF16),
            pltpu.VMEM((2, CL, NB), F32),
            pltpu.VMEM((2, NY, CW, NB), F32),
            pltpu.VMEM((2, CW, NB), F32),
            pltpu.VMEM((2, CW, NB), F32),
            pltpu.VMEM((2, NY, CW, NB), F32),
            pltpu.VMEM((2, CL, NB), F32),
            DMA((2,)),
            DMA((2,)),
            DMA((2, NH, NX)),
            DMA((2, NH, NX)),
            DMA((2, NH, NX)),
            DMA((2, NH, NX)),
            DMA,
            DMA,
            DMA((2, 2, FAR + 1, 2)),
            DMA((2, 2, FAR + 1, 2)),
            DMA((2, 2, FAR + 1, 2)),
            DMA((2, 2, FAR + 1, 2)),
            DMA((2, NY)),
            DMA((2, NY)),
            DMA((2, NY)),
            DMA((2,)),
            DMA((2,)),
            DMA((2, NY)),
            DMA((2, NY)),
            DMA,
            DMA,
        ],
        compiler_params=pltpu.CompilerParams(collective_id=0, has_side_effects=True),
    )(sweep_order, offsets, eigvecs, reflectors, factors)


def build(mesh, dims):
    placed = (
        P("row", "col"),
        P(None, "row", "col", None),
        P(None, "row", "col", None),
        P(None, "row"),
        P(),
    )
    return jax.shard_map(
        functools.partial(on_device, dims),
        mesh=mesh,
        in_specs=placed,
        out_specs=P("row", "col"),
        check_vma=False,
    )


def solution(mesh):
    return build(mesh, (Z_LO, Y, X, Z_HI, CORES))
```

```python
import functools

import jax
import jax.numpy as jnp
from jax import lax
from jax.experimental import pallas as pl
from jax.experimental.pallas import tpu as pltpu
from jax.sharding import PartitionSpec as P

MESH = pl.DeviceIdType.MESH
F32, BF16 = jnp.float32, jnp.bfloat16
NN, NT = ((1,), (0,)), ((1,), (1,))

Z_LO, Y, X, Z_HI, CORES = 4, 8, 4, 2, 2


def split(value):
    high = value.astype(BF16)
    return high, (value - high.astype(F32)).astype(BF16)


def dot(left, right, dims):
    return lax.dot_general(left, right, (dims, ((), ())), preferred_element_type=F32)


def product(left, right, dims):
    (lh, ll), (rh, rl) = left, right
    return dot(lh, rh, dims) + (dot(lh, rl, dims) + dot(ll, rh, dims))


def kernel(
    dims,
    order_ref,
    offs_ref,
    eig_ref,
    refl_ref,
    fact_ref,
    out_ref,
    vf,
    ops_h,
    ops_l,
    proj,
    below_raw,
    below,
    init,
    gains,
    gains_h,
    gains_l,
    d_out,
    d_in,
    carry_in,
    states_out,
    states_in,
    back_out,
    back_in,
    rest_out,
    rest_in,
    z_s,
    z_r,
    x_s,
    x_r,
    q_s,
    q_r,
    e_s,
    e_r,
    g_s,
    g_r,
    gq_s,
    gq_r,
    d_s,
    d_r,
    i_s,
    c_s,
    c_r,
    s_s,
    s_r,
    a_s,
    a_r,
    h_s,
    h_r,
    ax_s,
    ax_r,
    aq_s,
    aq_r,
):
    KZ, NY, NX, NH, NQ = dims
    NB = eig_ref.shape[0]
    CL = eig_ref.shape[1]
    CW = CL // NY
    RC = refl_ref.shape[2]
    HB = NB // 2
    SHARE = HB // NQ
    PART = SHARE // 2
    FAR = NY // 2
    BACK = NB // (NX * NQ)

    row, col = lax.axis_index("row"), lax.axis_index("col")
    k, y = row // NY, row % NY
    x, h, q = col // (NH * NQ), (col // NQ) % NH, col % NQ
    last_row = KZ * NY - 1

    def y_peer(d):
        return (k * NY + (y + d) % NY, col)

    def x_peer(d):
        return (row, ((x + d) % NX) * (NH * NQ) + h * NQ + q)

    z_peer = (row, x * (NH * NQ) + (1 - h) * NQ + q)
    sibling = (row, x * (NH * NQ) + h * NQ + (1 - q))
    up_group, down_group = (row - NY, col), (row + NY, col)
    up_row, down_row = (row - 1, col), (row + 1, col)

    def copy(src, dst, ssem, rsem, device):
        return pltpu.make_async_remote_copy(
            src_ref=src,
            dst_ref=dst,
            send_sem=ssem,
            recv_sem=rsem,
            device_id=device,
            device_id_type=MESH,
        )

    def arrived(dst, rsem):
        copy(dst, dst, z_s.at[0], rsem, sibling).wait_recv()

    barrier = pltpu.get_barrier_semaphore()

    def greet(device):
        pl.semaphore_signal(barrier, inc=1, device_id=device, device_id_type=MESH)

    greet(z_peer)
    greet(sibling)
    for d in range(1, NX):
        greet(x_peer(d))
    for d in range(1, NY):
        greet(y_peer(d))
    has_up, has_down = k > 0, k < KZ - 1
    first_y, final_y = y == 0, y == NY - 1

    @pl.when(has_up)
    def _():
        greet(up_group)

    @pl.when(has_down)
    def _():
        greet(down_group)

    @pl.when(has_up & first_y)
    def _():
        greet(up_row)

    @pl.when(has_down & final_y)
    def _():
        greet(down_row)

    def start_of(t):
        return offs_ref[order_ref[t]]

    for t in range(2):
        chosen = order_ref[t]
        raw = refl_ref[chosen, 0]
        start = (
            col * RC + start_of(t) + lax.broadcasted_iota(jnp.int32, (RC, NB), 0)
        )
        position = lax.broadcasted_iota(jnp.int32, (RC, NB), 1)
        upper, lower = raw[:, :NB], raw[:, NB:]
        packed = jnp.where(position + NB >= start, lower, jnp.zeros_like(lower))
        packed = jnp.where(position >= start, upper, packed)
        unit = (position == start) | (position + NB == start)
        vf[t, x, h, q, pl.ds(0, RC)] = jnp.where(unit, jnp.ones_like(packed), packed)
        vf[t, x, h, q, pl.ds(RC, RC)] = fact_ref[chosen, 0]

    expected = (
        2
        + (NX - 1)
        + (NY - 1)
        + has_up.astype(jnp.int32)
        + has_down.astype(jnp.int32)
        + (has_up & first_y).astype(jnp.int32)
        + (has_down & final_y).astype(jnp.int32)
    )
    pl.semaphore_wait(barrier, expected)

    def z_send(t):
        piece = vf.at[t, x, h, q]
        return copy(piece, piece, z_s.at[t], z_r.at[t], z_peer)

    def x_send(t, p, d):
        piece = vf.at[t, x, h if p == 0 else 1 - h, q]
        return copy(piece, piece, x_s.at[t], x_r.at[t, p, d], x_peer(d))

    def q_send(t, p, d):
        piece = vf.at[t, (x + NX - d) % NX, h if p == 0 else 1 - h, q]
        return copy(piece, piece, q_s.at[t], q_r.at[t], sibling)

    def x_take(t, p, d):
        piece = vf.at[t, (x + NX - d) % NX, h if p == 0 else 1 - h, q]
        arrived(piece, x_r.at[t, p, d])
        q_send(t, p, d).start()

    def q_take(t):
        arrived(vf.at[t, :, :, 0], q_r.at[t])

    def z_take(t):
        arrived(vf.at[t, x, 1 - h, q], z_r.at[t])
        for d in range(1, NX):
            x_send(t, 1, d).start()
        q_send(t, 1, 0).start()

    def e_send():
        return copy(eig_ref, below_raw, e_s, e_r, up_row)

    y_far_first = sorted(range(1, NY), key=lambda d: -min(d, NY - d))
    near_first = sorted(range(1, NX), key=lambda d: min(d, NX - d))
    for t in range(2):
        z_send(t).start()
    for t in range(2):
        for d in near_first:
            x_send(t, 0, d).start()
        q_send(t, 0, 0).start()

    @pl.when(row > 0)
    def _():
        e_send().start()

    def init_send(t, d):
        there = pl.ds(((y + d) % NY) * CW, CW)
        return copy(
            init.at[t, there], carry_in.at[t], i_s.at[t], c_r.at[t], y_peer(d)
        )

    def send_init(t):
        for d in range(1, NY):
            init_send(t, d).start()
        carry_in[t] = init[t, pl.ds(0, CW)]

    @pl.when(row == 0)
    def _():
        init[0] = jnp.transpose(eig_ref[...])
        send_init(0)

    z_take(0)
    for d in near_first:
        x_take(0, 0, d)
    z_take(1)
    for d in near_first:
        x_take(0, 1, d)

    @pl.when(row < last_row)
    def _():
        arrived(below_raw, e_r)
        below[0] = jnp.transpose(below_raw[...])

    @pl.when(row == last_row)
    def _():
        below[0] = jnp.zeros((CL, NB), F32)

    q_take(0)

    UP, LOW, FAC = 0, 1, 2

    def parts(t, which):
        return ops_h[t, which], ops_l[t, which]

    def unpack(t):
        both = vf[t, :, :, :, pl.ds(0, RC), :].reshape(NB, NB)
        factor = vf[t, :, :, :, pl.ds(RC, RC), :].reshape(NB, NB)
        start = lax.broadcasted_iota(jnp.int32, (NB, NB), 0) + start_of(t)
        position = lax.broadcasted_iota(jnp.int32, (NB, NB), 1)
        zero = jnp.zeros_like(both)
        for which, value in (
            (UP, jnp.where(position >= start, both, zero)),
            (LOW, jnp.where(position < start, both, zero)),
            (FAC, factor),
        ):
            ops_h[t, which], ops_l[t, which] = split(value)

    def make_gain(t):
        inner = product(parts(t, FAC), parts(t, UP), NN)
        turned = split(jnp.transpose(inner))
        gain = -product(turned, parts(t, LOW), NN)
        gains[t, y, :, :HB] = gain[:HB, :HB] + jnp.transpose(gain[HB:, HB:])
        gains[t, y, :, HB:] = gain[HB:, :HB]
        return turned

    def spread_gain(t, i):
        square, corner = gains[t, i, :, :HB], gains[t, i, :, HB:]
        down = lax.broadcasted_iota(jnp.int32, (HB, HB), 0)
        across = lax.broadcasted_iota(jnp.int32, (HB, HB), 1)
        zero = jnp.zeros_like(square)
        first = jnp.where(down > across, square, zero)
        second = jnp.transpose(jnp.where(across > down, square, zero))
        for r, c, value in (
            (0, 0, first),
            (0, 1, zero),
            (1, 0, corner),
            (1, 1, second),
        ):
            high, low = split(value)
            gains_h[t, i, r * HB : (r + 1) * HB, c * HB : (c + 1) * HB] = high
            gains_l[t, i, r * HB : (r + 1) * HB, c * HB : (c + 1) * HB] = low

    def make_shift(t):
        rows = below[t]
        lowered = product(split(rows), parts(t, LOW), NT)
        proj[t] = lowered
        coeffs = split(product(split(lowered), parts(t, FAC), NT))
        d_out[t] = rows - product(coeffs, parts(t, LOW), NN)
        return coeffs

    def make_back(turned, coeffs):
        down = lax.broadcasted_iota(jnp.int32, (NB, NB), 0)
        across = lax.broadcasted_iota(jnp.int32, (NB, NB), 1)
        unit = jnp.where(down == across, 1.0, 0.0).astype(F32)
        back_out[...] = unit - product(turned, parts(0, UP), NN)
        rest_out[...] = -product(coeffs, parts(0, UP), NN)

    def finish(t, rows):
        coeffs = product(split(rows), parts(t, UP), NT) + proj[t]
        coeffs = product(split(coeffs), parts(t, FAC), NT)
        return rows - product(split(coeffs), parts(t, UP), NN)

    def ring_ids():
        for d in range(1, FAR + 1):
            for m in range(2):
                for way in range(2):
                    if d < FAR or m == way:
                        yield way, d, m

    def part_rows(m, core):
        return pl.ds(pl.multiple_of(core * SHARE + m * PART, PART), PART)

    def ring_send(t, way, d, m):
        source = (y + NY - (d - 1)) % NY if way == 0 else (y + (d - 1)) % NY
        piece = gains.at[t, source, part_rows(m, q)]
        there = y_peer(1 if way == 0 else NY - 1)
        return copy(
            piece, piece, g_s.at[t], g_r.at[t, way, d - 1, m], there
        )

    def ring_source(way, d):
        return (y + NY - d) % NY if way == 0 else (y + d) % NY

    def ring_pass(t, way, d, m):
        piece = gains.at[t, ring_source(way, d), part_rows(m, q)]
        return copy(
            piece, piece, gq_s.at[t], gq_r.at[t, d - 1], sibling
        )

    def ring_start(t):
        for way, d, m in ring_ids():
            if d == 1:
                ring_send(t, way, d, m).start()

    def ring_step(t, distance):
        ids = list(ring_ids())
        for way, d, m in ids:
            if d != distance:
                continue
            arrived(
                gains.at[t, ring_source(way, d), part_rows(m, q)], g_r.at[t, way, d - 1, m]
            )
            if (way, d + 1, m) in ids:
                ring_send(t, way, d + 1, m).start()
            ring_pass(t, way, d, m).start()

    def ring_land(t, distance):
        pieces = 2 if distance == FAR else 4
        arrived(gains.at[t, 0, pl.ds(0, pieces * PART)], gq_r.at[t, distance - 1])
        for way in range(1 if distance == FAR else 2):
            spread_gain(t, ring_source(way, distance))

    def d_send(t, d):
        there = pl.ds(((y + d) % NY) * CW, CW)
        return copy(
            d_out.at[t, there], d_in.at[t, y], d_s.at[t], d_r.at[t], y_peer(d)
        )

    def send_shift(t):
        for d in y_far_first:
            d_send(t, d).start()
        d_in[t, y] = d_out[t, pl.ds(y * CW, CW)]

    def take_shift(t):
        arrived(d_in.at[t, pl.ds(0, NY - 1)], d_r.at[t])

    def owner_of(t, i):
        return i - 1 if t == 0 else i

    def state_send(t, i):
        return copy(
            states_out.at[t, i],
            states_in.at[t, pl.ds(y * CW, CW)],
            s_s.at[t],
            s_r.at[t],
            (k * NY + owner_of(t, i), col),
        )

    def share_state(t, i):
        if 0 <= owner_of(t, i) < NY:

            @pl.when(y != owner_of(t, i))
            def _():
                state_send(t, i).start()

    def carry_send(t):
        return copy(
            states_out.at[t, NY], carry_in.at[t], c_s.at[t], c_r.at[t], down_group
        )

    def chain(t):
        take_shift(t)

        @pl.when(row > 0)
        def _():
            arrived(carry_in.at[t], c_r.at[t])

        state = carry_in[t]
        for i in range(NY):
            states_out[t, i] = state
            share_state(t, i)
            high, low = split(state)
            gain_h = gains_h[t, i]
            pair = dot(jnp.concatenate([high, low], 0), gain_h, NN)
            state = (pair[:CW] + pair[CW:]) + (
                dot(high, gains_l[t, i], NN) + d_in[t, i]
            )
        states_out[t, NY] = state

        @pl.when(has_down)
        def _():
            carry_send(t).start()

        share_state(t, NY)

    def collect(t):
        mine = pl.ds(y * CW, CW)
        states_in[t, mine] = states_out[t, y + (1 - t)]
        arrived(states_in.at[t, pl.ds(0, (NY - 1) * CW)], s_r.at[t])

    def back_rows(column, core):
        at = (column * NQ + core) * BACK
        return pl.ds(pl.multiple_of(at, BACK), BACK)

    def a_send():
        rows = back_rows(x, q)
        return copy(back_out.at[rows], back_in.at[rows], a_s, a_r, up_row)

    def h_send():
        return copy(rest_out, rest_in, h_s, h_r, up_row)

    def ax_send(d):
        piece = back_in.at[back_rows(x, q)]
        return copy(piece, piece, ax_s, ax_r.at[d - 1], x_peer(d))

    def aq_send(d):
        piece = back_in.at[back_rows((x + NX - d) % NX, q)]
        return copy(piece, piece, aq_s, aq_r, sibling)

    def back_take():
        @pl.when(row < last_row)
        def _():
            arrived(back_in.at[back_rows(x, q)], a_r)
            for d in near_first:
                ax_send(d).start()
            aq_send(0).start()

    def back_pass():
        @pl.when(row < last_row)
        def _():
            for d in near_first:
                arrived(back_in.at[back_rows((x + NX - d) % NX, q)], ax_r.at[d - 1])
                aq_send(d).start()

    def back_land():
        arrived(back_in.at[pl.ds(0, NX * BACK)], aq_r)
        arrived(rest_in, h_r)

    def left(view, sem):
        copy(view, view, sem, z_r.at[0], sibling).wait_send()

    def left_early():
        for t in range(2):
            z_send(t).wait_send()
            left(vf.at[t, pl.ds(0, NX - 1), :, 0], x_s.at[t])
            left(vf.at[t, :, :, 0], q_s.at[t])

        @pl.when(row > 0)
        def _():
            e_send().wait_send()

    def left_ring(t):
        sent = gains.at[t, pl.ds(0, NY - 1), pl.ds(0, HB // 2)]
        left(sent, g_s.at[t])
        left(sent, gq_s.at[t])
        left(d_out.at[t, pl.ds(0, (NY - 1) * CW)], d_s.at[t])

    def left_back():
        @pl.when(row > 0)
        def _():
            a_send().wait_send()
            h_send().wait_send()

        @pl.when(row < last_row)
        def _():
            left(back_in.at[pl.ds(0, (NX - 1) * BACK)], ax_s)
            left(back_in.at[pl.ds(0, NX * BACK)], aq_s)

        @pl.when(row == 0)
        def _():
            for t in range(2):
                left(init.at[t, pl.ds(0, (NY - 1) * CW)], i_s.at[t])

    def left_states(t):
        left(states_out.at[t, pl.ds(0, NY - 1)], s_s.at[t])

        @pl.when(has_down)
        def _():
            carry_send(t).wait_send()

    unpack(0)
    turned = make_gain(0)
    ring_start(0)
    coeffs = make_shift(0)
    send_shift(0)
    spread_gain(0, y)
    make_back(turned, coeffs)

    def ring_slot(t, d):
        if d <= FAR:
            ring_step(t, d)
            if d > 1:
                ring_land(t, d - 1)
            if d == FAR:
                ring_land(t, d)

    for d in range(1, FAR + 1):
        ring_slot(0, d)

    @pl.when(row > 0)
    def _():
        a_send().start()
        h_send().start()

    def second_set():
        for p in range(2):
            for d in near_first:
                x_take(1, p, d)
        q_take(1)
        unpack(1)
        make_gain(1)
        ring_start(1)
        spread_gain(1, y)

    @pl.when(k >= 1)
    def _():
        second_set()

    @pl.when(k >= 2)
    def _():
        back_take()
        ring_slot(1, 1)
        back_pass()

    @pl.when(k >= 3)
    def _():
        ring_slot(1, 2)

    chain(0)

    @pl.when(k < 1)
    def _():
        second_set()

    @pl.when(k < 2)
    def _():
        back_take()
        ring_slot(1, 1)
        back_pass()

    @pl.when(k == 2)
    def _():
        ring_slot(1, 2)

    @pl.when(k >= 3)
    def _():
        ring_slot(1, 3)

    left_early()
    left_ring(0)
    collect(0)

    @pl.when(row < last_row)
    def _():
        back_land()
        below[1] = rest_in[...] + product(
            split(states_in[0]), split(back_in[...]), NN
        )

    @pl.when(row == last_row)
    def _():
        below[1] = jnp.zeros((CL, NB), F32)

    make_shift(1)
    send_shift(1)

    @pl.when(row == 0)
    def _():
        init[1] = finish(0, init[0])
        send_init(1)

    @pl.when(k < 2)
    def _():
        ring_slot(1, 2)

    @pl.when(k < 3)
    def _():
        ring_slot(1, 3)

    for d in range(4, FAR + 1):
        ring_slot(1, d)
    chain(1)
    left_ring(1)
    left_states(0)
    left_back()
    collect(1)
    out_ref[...] = jnp.transpose(finish(1, states_in[1]))
    left_states(1)


def on_device(dims, eigvecs, reflectors, factors, offsets, sweep_order):
    KZ, NY, NX, NH, NQ = dims
    NB, CL = eigvecs.shape
    CW = CL // NY
    RC = reflectors.shape[2]
    FAR = NY // 2
    DMA = pltpu.SemaphoreType.DMA
    vmem = pl.BlockSpec(memory_space=pltpu.VMEM)
    smem = pl.BlockSpec(memory_space=pltpu.SMEM)
    return pl.pallas_call(
        functools.partial(kernel, dims),
        out_shape=jax.ShapeDtypeStruct((NB, CL), F32),
        in_specs=[smem, smem, vmem, vmem, vmem],
        out_specs=vmem,
        scratch_shapes=[
            pltpu.VMEM((2, NX, NH, NQ, 2 * RC, NB), F32),
            pltpu.VMEM((2, 3, NB, NB), BF16),
            pltpu.VMEM((2, 3, NB, NB), BF16),
            pltpu.VMEM((2, CL, NB), F32),
            pltpu.VMEM((NB, CL), F32),
            pltpu.VMEM((2, CL, NB), F32),
            pltpu.VMEM((2, CL, NB), F32),
            pltpu.VMEM((2, NY, NB // 2, NB), F32),
            pltpu.VMEM((2, NY, NB, NB), BF16),
            pltpu.VMEM((2, NY, NB, NB), BF16),
            pltpu.VMEM((2, CL, NB), F32),
            pltpu.VMEM((2, NY, CW, NB), F32),
            pltpu.VMEM((2, CW, NB), F32),
            pltpu.VMEM((2, NY + 1, CW, NB), F32),
            pltpu.VMEM((2, CL, NB), F32),
            pltpu.VMEM((NB, NB), F32),
            pltpu.VMEM((NB, NB), F32),
            pltpu.VMEM((CL, NB), F32),
            pltpu.VMEM((CL, NB), F32),
            DMA((2,)),
            DMA((2,)),
            DMA((2,)),
            DMA((2, NH, NX)),
            DMA((2,)),
            DMA((2,)),
            DMA,
            DMA,
            DMA((2,)),
            DMA((2, 2, FAR, 2)),
            DMA((2,)),
            DMA((2, FAR)),
            DMA((2,)),
            DMA((2,)),
            DMA((2,)),
            DMA((2,)),
            DMA((2,)),
            DMA((2,)),
            DMA((2,)),
            DMA,
            DMA,
            DMA,
            DMA,
            DMA,
            DMA((NX - 1,)),
            DMA,
            DMA,
        ],
        compiler_params=pltpu.CompilerParams(collective_id=0, has_side_effects=True),
    )(sweep_order, offsets.reshape(-1), eigvecs, reflectors, factors)


def build(mesh, dims):
    placed = (
        P("row", "col"),
        P(None, "row", "col", None),
        P(None, "row", "col", None),
        P(None, "row"),
        P(),
    )
    return jax.shard_map(
        functools.partial(on_device, dims),
        mesh=mesh,
        in_specs=placed,
        out_specs=P("row", "col"),
        check_vma=False,
    )


def solution(mesh):
    return build(mesh, (Z_LO, Y, X, Z_HI, CORES))
```

```python
import functools

import jax
import jax.numpy as jnp
from jax import lax
from jax.experimental import pallas as pl
from jax.experimental.pallas import tpu as pltpu
from jax.sharding import PartitionSpec as P

MESH = pl.DeviceIdType.MESH
F32, BF16 = jnp.float32, jnp.bfloat16
NN, NT = ((1,), (0,)), ((1,), (1,))

Z_LO, Y, X, Z_HI, CORES = 4, 8, 4, 2, 2


def split(value):
    high = value.astype(BF16)
    return high, (value - high.astype(F32)).astype(BF16)


def dot(left, right, dims):
    return lax.dot_general(left, right, (dims, ((), ())), preferred_element_type=F32)


def product(left, right, dims):
    (lh, ll), (rh, rl) = left, right
    return dot(lh, rh, dims) + (dot(lh, rl, dims) + dot(ll, rh, dims))


def kernel(
    dims,
    order_hbm,
    offs_hbm,
    eig_hbm,
    refl_hbm,
    fact_hbm,
    out_hbm,
    order_ref,
    offs_ref,
    eig_ref,
    refl_ref,
    fact_ref,
    out_ref,
    own_s,
    vf,
    ops_h,
    ops_l,
    proj,
    below_raw,
    below,
    init,
    gains,
    gains_h,
    gains_l,
    d_out,
    d_in,
    carry_in,
    states_out,
    states_in,
    back_out,
    back_in,
    rest_out,
    rest_in,
    z_s,
    z_r,
    x_s,
    x_r,
    q_s,
    q_r,
    e_s,
    e_r,
    g_s,
    g_r,
    gq_s,
    gq_r,
    d_s,
    d_r,
    i_s,
    c_s,
    c_r,
    s_s,
    s_r,
    a_s,
    a_r,
    h_s,
    h_r,
    ax_s,
    ax_r,
    aq_s,
    aq_r,
):
    KZ, NY, NX, NH, NQ = dims
    NB = eig_ref.shape[0]
    CL = eig_ref.shape[1]
    CW = CL // NY
    RC = refl_ref.shape[2]
    HB = NB // 2
    SHARE = HB // NQ
    PART = SHARE // 2
    FAR = NY // 2
    BACK = NB // (NX * NQ)

    row, col = lax.axis_index("row"), lax.axis_index("col")
    k, y = row // NY, row % NY
    x, h, q = col // (NH * NQ), (col // NQ) % NH, col % NQ
    last_row = KZ * NY - 1

    def y_peer(d):
        return (k * NY + (y + d) % NY, col)

    def x_peer(d):
        return (row, ((x + d) % NX) * (NH * NQ) + h * NQ + q)

    z_peer = (row, x * (NH * NQ) + (1 - h) * NQ + q)
    sibling = (row, x * (NH * NQ) + h * NQ + (1 - q))
    up_group, down_group = (row - NY, col), (row + NY, col)
    up_row, down_row = (row - 1, col), (row + 1, col)

    def copy(src, dst, ssem, rsem, device):
        return pltpu.make_async_remote_copy(
            src_ref=src,
            dst_ref=dst,
            send_sem=ssem,
            recv_sem=rsem,
            device_id=device,
            device_id_type=MESH,
        )

    def arrived(dst, rsem):
        copy(dst, dst, z_s.at[0], rsem, sibling).wait_recv()

    loads = [
        pltpu.make_async_copy(order_hbm, order_ref, own_s.at[4]),
        pltpu.make_async_copy(offs_hbm, offs_ref, own_s.at[5]),
        pltpu.make_async_copy(refl_hbm, refl_ref, own_s.at[0]),
        pltpu.make_async_copy(fact_hbm, fact_ref, own_s.at[1]),
        pltpu.make_async_copy(eig_hbm, eig_ref, own_s.at[2]),
    ]
    for load in loads:
        load.start()

    barrier = pltpu.get_barrier_semaphore()

    def greet(device):
        pl.semaphore_signal(barrier, inc=1, device_id=device, device_id_type=MESH)

    greet(z_peer)
    greet(sibling)
    for d in range(1, NX):
        greet(x_peer(d))
    for d in range(1, NY):
        greet(y_peer(d))
    has_up, has_down = k > 0, k < KZ - 1
    first_y, final_y = y == 0, y == NY - 1

    @pl.when(has_up)
    def _():
        greet(up_group)

    @pl.when(has_down)
    def _():
        greet(down_group)

    @pl.when(has_up & first_y)
    def _():
        greet(up_row)

    @pl.when(has_down & final_y)
    def _():
        greet(down_row)

    for load in loads[:4]:
        load.wait()

    def start_of(t):
        return offs_ref[order_ref[t]]

    for t in range(2):
        chosen = order_ref[t]
        raw = refl_ref[chosen, 0]
        start = (
            col * RC + start_of(t) + lax.broadcasted_iota(jnp.int32, (RC, NB), 0)
        )
        position = lax.broadcasted_iota(jnp.int32, (RC, NB), 1)
        upper, lower = raw[:, :NB], raw[:, NB:]
        packed = jnp.where(position + NB >= start, lower, jnp.zeros_like(lower))
        packed = jnp.where(position >= start, upper, packed)
        unit = (position == start) | (position + NB == start)
        vf[t, x, h, q, pl.ds(0, RC)] = jnp.where(unit, jnp.ones_like(packed), packed)
        vf[t, x, h, q, pl.ds(RC, RC)] = fact_ref[chosen, 0]

    expected = (
        2
        + (NX - 1)
        + (NY - 1)
        + has_up.astype(jnp.int32)
        + has_down.astype(jnp.int32)
        + (has_up & first_y).astype(jnp.int32)
        + (has_down & final_y).astype(jnp.int32)
    )
    pl.semaphore_wait(barrier, expected)

    def z_send(t):
        piece = vf.at[t, x, h, q]
        return copy(piece, piece, z_s.at[t], z_r.at[t], z_peer)

    def x_send(t, p, d):
        piece = vf.at[t, x, h if p == 0 else 1 - h, q]
        return copy(piece, piece, x_s.at[t], x_r.at[t, p, d], x_peer(d))

    def q_send(t, p, d):
        piece = vf.at[t, (x + NX - d) % NX, h if p == 0 else 1 - h, q]
        return copy(piece, piece, q_s.at[t], q_r.at[t], sibling)

    def x_take(t, p, d):
        piece = vf.at[t, (x + NX - d) % NX, h if p == 0 else 1 - h, q]
        arrived(piece, x_r.at[t, p, d])
        q_send(t, p, d).start()

    def q_take(t):
        arrived(vf.at[t, :, :, 0], q_r.at[t])

    def z_take(t):
        arrived(vf.at[t, x, 1 - h, q], z_r.at[t])
        for d in range(1, NX):
            x_send(t, 1, d).start()
        q_send(t, 1, 0).start()

    def e_send():
        return copy(eig_ref, below_raw, e_s, e_r, up_row)

    y_far_first = sorted(range(1, NY), key=lambda d: -min(d, NY - d))
    near_first = sorted(range(1, NX), key=lambda d: min(d, NX - d))
    for t in range(2):
        z_send(t).start()
    for t in range(2):
        for d in near_first:
            x_send(t, 0, d).start()
        q_send(t, 0, 0).start()

    loads[4].wait()

    @pl.when(row > 0)
    def _():
        e_send().start()

    def init_send(t, d):
        there = pl.ds(((y + d) % NY) * CW, CW)
        return copy(
            init.at[t, there], carry_in.at[t], i_s.at[t], c_r.at[t], y_peer(d)
        )

    def send_init(t):
        for d in range(1, NY):
            init_send(t, d).start()
        carry_in[t] = init[t, pl.ds(0, CW)]

    @pl.when(row == 0)
    def _():
        init[0] = jnp.transpose(eig_ref[...])
        send_init(0)

    z_take(0)
    for d in near_first:
        x_take(0, 0, d)
    z_take(1)
    for d in near_first:
        x_take(0, 1, d)

    @pl.when(row < last_row)
    def _():
        arrived(below_raw, e_r)
        below[0] = jnp.transpose(below_raw[...])

    @pl.when(row == last_row)
    def _():
        below[0] = jnp.zeros((CL, NB), F32)

    q_take(0)

    UP, LOW, FAC = 0, 1, 2

    def parts(t, which):
        return ops_h[t, which], ops_l[t, which]

    def unpack(t):
        both = vf[t, :, :, :, pl.ds(0, RC), :].reshape(NB, NB)
        factor = vf[t, :, :, :, pl.ds(RC, RC), :].reshape(NB, NB)
        start = lax.broadcasted_iota(jnp.int32, (NB, NB), 0) + start_of(t)
        position = lax.broadcasted_iota(jnp.int32, (NB, NB), 1)
        zero = jnp.zeros_like(both)
        for which, value in (
            (UP, jnp.where(position >= start, both, zero)),
            (LOW, jnp.where(position < start, both, zero)),
            (FAC, factor),
        ):
            ops_h[t, which], ops_l[t, which] = split(value)

    def make_gain(t):
        inner = product(parts(t, FAC), parts(t, UP), NN)
        turned = split(jnp.transpose(inner))
        gain = -product(turned, parts(t, LOW), NN)
        gains[t, y, :, :HB] = gain[:HB, :HB] + jnp.transpose(gain[HB:, HB:])
        gains[t, y, :, HB:] = gain[HB:, :HB]
        return turned

    def spread_gain(t, i):
        square, corner = gains[t, i, :, :HB], gains[t, i, :, HB:]
        down = lax.broadcasted_iota(jnp.int32, (HB, HB), 0)
        across = lax.broadcasted_iota(jnp.int32, (HB, HB), 1)
        zero = jnp.zeros_like(square)
        first = jnp.where(down > across, square, zero)
        second = jnp.transpose(jnp.where(across > down, square, zero))
        for r, c, value in (
            (0, 0, first),
            (0, 1, zero),
            (1, 0, corner),
            (1, 1, second),
        ):
            high, low = split(value)
            gains_h[t, i, r * HB : (r + 1) * HB, c * HB : (c + 1) * HB] = high
            gains_l[t, i, r * HB : (r + 1) * HB, c * HB : (c + 1) * HB] = low

    def make_shift(t):
        rows = below[t]
        lowered = product(split(rows), parts(t, LOW), NT)
        proj[t] = lowered
        coeffs = split(product(split(lowered), parts(t, FAC), NT))
        d_out[t] = rows - product(coeffs, parts(t, LOW), NN)
        return coeffs

    def make_back(turned, coeffs):
        down = lax.broadcasted_iota(jnp.int32, (NB, NB), 0)
        across = lax.broadcasted_iota(jnp.int32, (NB, NB), 1)
        unit = jnp.where(down == across, 1.0, 0.0).astype(F32)
        back_out[...] = unit - product(turned, parts(0, UP), NN)
        rest_out[...] = -product(coeffs, parts(0, UP), NN)

    def finish(t, rows):
        coeffs = product(split(rows), parts(t, UP), NT) + proj[t]
        coeffs = product(split(coeffs), parts(t, FAC), NT)
        return rows - product(split(coeffs), parts(t, UP), NN)

    def ring_ids():
        for d in range(1, FAR + 1):
            for m in range(2):
                for way in range(2):
                    if d < FAR or m == way:
                        yield way, d, m

    def part_rows(m, core):
        return pl.ds(pl.multiple_of(core * SHARE + m * PART, PART), PART)

    def ring_send(t, way, d, m):
        source = (y + NY - (d - 1)) % NY if way == 0 else (y + (d - 1)) % NY
        piece = gains.at[t, source, part_rows(m, q)]
        there = y_peer(1 if way == 0 else NY - 1)
        return copy(
            piece, piece, g_s.at[t], g_r.at[t, way, d - 1, m], there
        )

    def ring_source(way, d):
        return (y + NY - d) % NY if way == 0 else (y + d) % NY

    def ring_pass(t, way, d, m):
        piece = gains.at[t, ring_source(way, d), part_rows(m, q)]
        return copy(
            piece, piece, gq_s.at[t], gq_r.at[t, d - 1], sibling
        )

    def ring_start(t):
        for way, d, m in ring_ids():
            if d == 1:
                ring_send(t, way, d, m).start()

    def ring_step(t, distance):
        ids = list(ring_ids())
        for way, d, m in ids:
            if d != distance:
                continue
            arrived(
                gains.at[t, ring_source(way, d), part_rows(m, q)], g_r.at[t, way, d - 1, m]
            )
            if (way, d + 1, m) in ids:
                ring_send(t, way, d + 1, m).start()
            ring_pass(t, way, d, m).start()

    def ring_land(t, distance):
        pieces = 2 if distance == FAR else 4
        arrived(gains.at[t, 0, pl.ds(0, pieces * PART)], gq_r.at[t, distance - 1])
        for way in range(1 if distance == FAR else 2):
            spread_gain(t, ring_source(way, distance))

    def d_send(t, d):
        there = pl.ds(((y + d) % NY) * CW, CW)
        return copy(
            d_out.at[t, there], d_in.at[t, y], d_s.at[t], d_r.at[t], y_peer(d)
        )

    def send_shift(t):
        for d in y_far_first:
            d_send(t, d).start()
        d_in[t, y] = d_out[t, pl.ds(y * CW, CW)]

    def take_shift(t):
        arrived(d_in.at[t, pl.ds(0, NY - 1)], d_r.at[t])

    def owner_of(t, i):
        return i - 1 if t == 0 else i

    def state_send(t, i):
        return copy(
            states_out.at[t, i],
            states_in.at[t, pl.ds(y * CW, CW)],
            s_s.at[t],
            s_r.at[t],
            (k * NY + owner_of(t, i), col),
        )

    def share_state(t, i):
        if 0 <= owner_of(t, i) < NY:

            @pl.when(y != owner_of(t, i))
            def _():
                state_send(t, i).start()

    def carry_send(t):
        return copy(
            states_out.at[t, NY], carry_in.at[t], c_s.at[t], c_r.at[t], down_group
        )

    def chain(t):
        take_shift(t)

        @pl.when(row > 0)
        def _():
            arrived(carry_in.at[t], c_r.at[t])

        state = carry_in[t]
        for i in range(NY):
            states_out[t, i] = state
            share_state(t, i)
            high, low = split(state)
            gain_h = gains_h[t, i]
            pair = dot(jnp.concatenate([high, low], 0), gain_h, NN)
            state = (pair[:CW] + pair[CW:]) + (
                dot(high, gains_l[t, i], NN) + d_in[t, i]
            )
        states_out[t, NY] = state

        @pl.when(has_down)
        def _():
            carry_send(t).start()

        share_state(t, NY)

    def collect(t):
        mine = pl.ds(y * CW, CW)
        states_in[t, mine] = states_out[t, y + (1 - t)]
        arrived(states_in.at[t, pl.ds(0, (NY - 1) * CW)], s_r.at[t])

    def back_rows(column, core):
        at = (column * NQ + core) * BACK
        return pl.ds(pl.multiple_of(at, BACK), BACK)

    def a_send():
        rows = back_rows(x, q)
        return copy(back_out.at[rows], back_in.at[rows], a_s, a_r, up_row)

    def h_send():
        return copy(rest_out, rest_in, h_s, h_r, up_row)

    def ax_send(d):
        piece = back_in.at[back_rows(x, q)]
        return copy(piece, piece, ax_s, ax_r.at[d - 1], x_peer(d))

    def aq_send(d):
        piece = back_in.at[back_rows((x + NX - d) % NX, q)]
        return copy(piece, piece, aq_s, aq_r, sibling)

    def back_take():
        @pl.when(row < last_row)
        def _():
            arrived(back_in.at[back_rows(x, q)], a_r)
            for d in near_first:
                ax_send(d).start()
            aq_send(0).start()

    def back_pass():
        @pl.when(row < last_row)
        def _():
            for d in near_first:
                arrived(back_in.at[back_rows((x + NX - d) % NX, q)], ax_r.at[d - 1])
                aq_send(d).start()

    def back_land():
        arrived(back_in.at[pl.ds(0, NX * BACK)], aq_r)
        arrived(rest_in, h_r)

    def left(view, sem):
        copy(view, view, sem, z_r.at[0], sibling).wait_send()

    def left_early():
        for t in range(2):
            z_send(t).wait_send()
            left(vf.at[t, pl.ds(0, NX - 1), :, 0], x_s.at[t])
            left(vf.at[t, :, :, 0], q_s.at[t])

        @pl.when(row > 0)
        def _():
            e_send().wait_send()

    def left_ring(t):
        sent = gains.at[t, pl.ds(0, NY - 1), pl.ds(0, HB // 2)]
        left(sent, g_s.at[t])
        left(sent, gq_s.at[t])
        left(d_out.at[t, pl.ds(0, (NY - 1) * CW)], d_s.at[t])

    def left_back():
        @pl.when(row > 0)
        def _():
            a_send().wait_send()
            h_send().wait_send()

        @pl.when(row < last_row)
        def _():
            left(back_in.at[pl.ds(0, (NX - 1) * BACK)], ax_s)
            left(back_in.at[pl.ds(0, NX * BACK)], aq_s)

        @pl.when(row == 0)
        def _():
            for t in range(2):
                left(init.at[t, pl.ds(0, (NY - 1) * CW)], i_s.at[t])

    def left_states(t):
        left(states_out.at[t, pl.ds(0, NY - 1)], s_s.at[t])

        @pl.when(has_down)
        def _():
            carry_send(t).wait_send()

    unpack(0)
    turned = make_gain(0)
    ring_start(0)
    coeffs = make_shift(0)
    send_shift(0)
    spread_gain(0, y)
    make_back(turned, coeffs)

    def ring_slot(t, d):
        if d <= FAR:
            ring_step(t, d)
            if d > 1:
                ring_land(t, d - 1)
            if d == FAR:
                ring_land(t, d)

    def second_vectors():
        q_take(1)
        unpack(1)

    def second_gain():
        make_gain(1)
        spread_gain(1, y)

    @pl.when(row > 0)
    def _():
        a_send().start()

    ring_step(0, 1)
    for p in range(2):
        for d in near_first:
            x_take(1, p, d)
    second_vectors()
    ring_step(0, 2)
    ring_land(0, 1)
    back_take()
    second_gain()
    for d in range(3, FAR + 1):
        ring_slot(0, d)
    if FAR == 2:
        ring_land(0, FAR)
    ring_start(1)
    back_pass()

    def rest_send():
        @pl.when(row > 0)
        def _():
            h_send().start()

    @pl.when(k >= 1)
    def _():
        rest_send()

    @pl.when(k >= 2)
    def _():
        ring_slot(1, 1)
        ring_slot(1, 2)

    @pl.when(k >= 3)
    def _():
        ring_slot(1, 3)

    chain(0)

    @pl.when(k < 1)
    def _():
        rest_send()

    @pl.when(k < 2)
    def _():
        ring_slot(1, 1)
        ring_slot(1, 2)

    @pl.when(k == 2)
    def _():
        ring_slot(1, 3)

    @pl.when(k >= 3)
    def _():
        ring_slot(1, 4)

    left_early()
    left_ring(0)
    collect(0)

    @pl.when(row < last_row)
    def _():
        back_land()
        below[1] = rest_in[...] + product(
            split(states_in[0]), split(back_in[...]), NN
        )

    @pl.when(row == last_row)
    def _():
        below[1] = jnp.zeros((CL, NB), F32)

    make_shift(1)
    send_shift(1)

    @pl.when(row == 0)
    def _():
        init[1] = finish(0, init[0])
        send_init(1)

    @pl.when(k < 2)
    def _():
        ring_slot(1, 3)

    @pl.when(k < 3)
    def _():
        ring_slot(1, 4)

    for d in range(5, FAR + 1):
        ring_slot(1, d)
    chain(1)
    left_ring(1)
    left_states(0)
    left_back()
    collect(1)
    out_ref[...] = jnp.transpose(finish(1, states_in[1]))
    store = pltpu.make_async_copy(out_ref, out_hbm, own_s.at[3])
    store.start()
    left_states(1)
    store.wait()


def on_device(dims, eigvecs, reflectors, factors, offsets, sweep_order):
    KZ, NY, NX, NH, NQ = dims
    NB, CL = eigvecs.shape
    CW = CL // NY
    RC = reflectors.shape[2]
    FAR = NY // 2
    DMA = pltpu.SemaphoreType.DMA
    hbm = pl.BlockSpec(memory_space=pltpu.HBM)
    return pl.pallas_call(
        functools.partial(kernel, dims),
        out_shape=jax.ShapeDtypeStruct((NB, CL), F32),
        in_specs=[hbm] * 5,
        out_specs=pl.BlockSpec(memory_space=pl.ANY),
        scratch_shapes=[
            pltpu.SMEM(sweep_order.shape, jnp.int32),
            pltpu.SMEM((offsets.shape[0],), jnp.int32),
            pltpu.VMEM(eigvecs.shape, F32),
            pltpu.VMEM(reflectors.shape, F32),
            pltpu.VMEM(factors.shape, F32),
            pltpu.VMEM(eigvecs.shape, F32),
            DMA((6,)),
            pltpu.VMEM((2, NX, NH, NQ, 2 * RC, NB), F32),
            pltpu.VMEM((2, 3, NB, NB), BF16),
            pltpu.VMEM((2, 3, NB, NB), BF16),
            pltpu.VMEM((2, CL, NB), F32),
            pltpu.VMEM((NB, CL), F32),
            pltpu.VMEM((2, CL, NB), F32),
            pltpu.VMEM((2, CL, NB), F32),
            pltpu.VMEM((2, NY, NB // 2, NB), F32),
            pltpu.VMEM((2, NY, NB, NB), BF16),
            pltpu.VMEM((2, NY, NB, NB), BF16),
            pltpu.VMEM((2, CL, NB), F32),
            pltpu.VMEM((2, NY, CW, NB), F32),
            pltpu.VMEM((2, CW, NB), F32),
            pltpu.VMEM((2, NY + 1, CW, NB), F32),
            pltpu.VMEM((2, CL, NB), F32),
            pltpu.VMEM((NB, NB), F32),
            pltpu.VMEM((NB, NB), F32),
            pltpu.VMEM((CL, NB), F32),
            pltpu.VMEM((CL, NB), F32),
            DMA((2,)),
            DMA((2,)),
            DMA((2,)),
            DMA((2, NH, NX)),
            DMA((2,)),
            DMA((2,)),
            DMA,
            DMA,
            DMA((2,)),
            DMA((2, 2, FAR, 2)),
            DMA((2,)),
            DMA((2, FAR)),
            DMA((2,)),
            DMA((2,)),
            DMA((2,)),
            DMA((2,)),
            DMA((2,)),
            DMA((2,)),
            DMA((2,)),
            DMA,
            DMA,
            DMA,
            DMA,
            DMA,
            DMA((NX - 1,)),
            DMA,
            DMA,
        ],
        compiler_params=pltpu.CompilerParams(
            collective_id=0, has_side_effects=True, vmem_limit_bytes=24 << 20
        ),
    )(
        *(
            pltpu.with_memory_space_constraint(part, pltpu.HBM)
            for part in (
                sweep_order,
                offsets.reshape(-1),
                eigvecs,
                reflectors,
                factors,
            )
        ),
    )


def build(mesh, dims):
    placed = (
        P("row", "col"),
        P(None, "row", "col", None),
        P(None, "row", "col", None),
        P(None, "row"),
        P(),
    )
    return jax.shard_map(
        functools.partial(on_device, dims),
        mesh=mesh,
        in_specs=placed,
        out_specs=P("row", "col"),
        check_vma=False,
    )


def solution(mesh):
    return build(mesh, (Z_LO, Y, X, Z_HI, CORES))
```

```python
import functools

import jax
import jax.numpy as jnp
from jax import lax
from jax.experimental import pallas as pl
from jax.experimental.pallas import tpu as pltpu
from jax.sharding import PartitionSpec as P

MESH = pl.DeviceIdType.MESH
F32, BF16 = jnp.float32, jnp.bfloat16
NN, NT = ((1,), (0,)), ((1,), (1,))

Z_LO, Y, X, Z_HI, CORES = 4, 8, 4, 2, 2


def split(value):
    high = value.astype(BF16)
    return high, (value - high.astype(F32)).astype(BF16)


def dot(left, right, dims):
    return lax.dot_general(left, right, (dims, ((), ())), preferred_element_type=F32)


def product(left, right, dims):
    (lh, ll), (rh, rl) = left, right
    return dot(lh, rh, dims) + (dot(lh, rl, dims) + dot(ll, rh, dims))


def kernel(
    dims,
    order_hbm,
    offs_hbm,
    eig_hbm,
    refl_hbm,
    fact_hbm,
    out_hbm,
    order_ref,
    offs_ref,
    eig_ref,
    refl_ref,
    fact_ref,
    out_ref,
    own_s,
    vf,
    ops_h,
    ops_l,
    proj,
    below_raw,
    below,
    init,
    gains,
    gains_h,
    gains_l,
    d_out,
    d_in,
    carry_in,
    states_out,
    states_in,
    back_out,
    back_in,
    rest_out,
    rest_in,
    z_s,
    z_r,
    x_s,
    x_r,
    q_s,
    q_r,
    e_s,
    e_r,
    g_s,
    g_r,
    gx_s,
    gx_r,
    gq_s,
    gq_r,
    d_s,
    d_r,
    i_s,
    c_s,
    c_r,
    s_s,
    s_r,
    a_s,
    a_r,
    h_s,
    h_r,
    ax_s,
    ax_r,
    aq_s,
    aq_r,
):
    KZ, NY, NX, NH, NQ = dims
    NB = eig_ref.shape[0]
    CL = eig_ref.shape[1]
    CW = CL // NY
    RC = refl_ref.shape[2]
    HB = NB // 2
    SHARE = HB // NQ
    PART = SHARE // NX
    BACK = NB // (NX * NQ)

    row, col = lax.axis_index("row"), lax.axis_index("col")
    k, y = row // NY, row % NY
    x, h, q = col // (NH * NQ), (col // NQ) % NH, col % NQ
    last_row = KZ * NY - 1

    def y_peer(d):
        return (k * NY + (y + d) % NY, col)

    def x_peer(d):
        return (row, ((x + d) % NX) * (NH * NQ) + h * NQ + q)

    z_peer = (row, x * (NH * NQ) + (1 - h) * NQ + q)
    sibling = (row, x * (NH * NQ) + h * NQ + (1 - q))
    up_group, down_group = (row - NY, col), (row + NY, col)
    up_row, down_row = (row - 1, col), (row + 1, col)

    def copy(src, dst, ssem, rsem, device):
        return pltpu.make_async_remote_copy(
            src_ref=src,
            dst_ref=dst,
            send_sem=ssem,
            recv_sem=rsem,
            device_id=device,
            device_id_type=MESH,
        )

    def arrived(dst, rsem):
        copy(dst, dst, z_s.at[0], rsem, sibling).wait_recv()

    loads = [
        pltpu.make_async_copy(order_hbm, order_ref, own_s.at[4]),
        pltpu.make_async_copy(offs_hbm, offs_ref, own_s.at[5]),
        pltpu.make_async_copy(refl_hbm, refl_ref, own_s.at[0]),
        pltpu.make_async_copy(fact_hbm, fact_ref, own_s.at[1]),
        pltpu.make_async_copy(eig_hbm, eig_ref, own_s.at[2]),
    ]
    for load in loads:
        load.start()

    barrier = pltpu.get_barrier_semaphore()

    def greet(device):
        pl.semaphore_signal(barrier, inc=1, device_id=device, device_id_type=MESH)

    greet(z_peer)
    greet(sibling)
    for d in range(1, NX):
        greet(x_peer(d))
    for d in range(1, NY):
        greet(y_peer(d))
    has_up, has_down = k > 0, k < KZ - 1
    first_y, final_y = y == 0, y == NY - 1

    @pl.when(has_up)
    def _():
        greet(up_group)

    @pl.when(has_down)
    def _():
        greet(down_group)

    @pl.when(has_up & first_y)
    def _():
        greet(up_row)

    @pl.when(has_down & final_y)
    def _():
        greet(down_row)

    for load in loads[:4]:
        load.wait()

    def start_of(t):
        return offs_ref[order_ref[t]]

    for t in range(2):
        chosen = order_ref[t]
        raw = refl_ref[chosen, 0]
        start = (
            col * RC + start_of(t) + lax.broadcasted_iota(jnp.int32, (RC, NB), 0)
        )
        position = lax.broadcasted_iota(jnp.int32, (RC, NB), 1)
        upper, lower = raw[:, :NB], raw[:, NB:]
        packed = jnp.where(position + NB >= start, lower, jnp.zeros_like(lower))
        packed = jnp.where(position >= start, upper, packed)
        unit = (position == start) | (position + NB == start)
        vf[t, x, h, q, pl.ds(0, RC)] = jnp.where(unit, jnp.ones_like(packed), packed)
        vf[t, x, h, q, pl.ds(RC, RC)] = fact_ref[chosen, 0]

    expected = (
        2
        + (NX - 1)
        + (NY - 1)
        + has_up.astype(jnp.int32)
        + has_down.astype(jnp.int32)
        + (has_up & first_y).astype(jnp.int32)
        + (has_down & final_y).astype(jnp.int32)
    )
    pl.semaphore_wait(barrier, expected)

    def z_send(t):
        piece = vf.at[t, x, h, q]
        return copy(piece, piece, z_s.at[t], z_r.at[t], z_peer)

    def x_send(t, p, d):
        piece = vf.at[t, x, h if p == 0 else 1 - h, q]
        return copy(piece, piece, x_s.at[t], x_r.at[t, p, d], x_peer(d))

    def q_send(t, p, d):
        piece = vf.at[t, (x + NX - d) % NX, h if p == 0 else 1 - h, q]
        return copy(piece, piece, q_s.at[t], q_r.at[t], sibling)

    def x_take(t, p, d):
        piece = vf.at[t, (x + NX - d) % NX, h if p == 0 else 1 - h, q]
        arrived(piece, x_r.at[t, p, d])
        q_send(t, p, d).start()

    def q_take(t):
        arrived(vf.at[t, :, :, 0], q_r.at[t])

    def z_take(t):
        arrived(vf.at[t, x, 1 - h, q], z_r.at[t])
        for d in range(1, NX):
            x_send(t, 1, d).start()
        q_send(t, 1, 0).start()

    def e_send():
        return copy(eig_ref, below_raw, e_s, e_r, up_row)

    y_near_first = sorted(range(1, NY), key=lambda d: min(d, NY - d))
    y_far_first = sorted(range(1, NY), key=lambda d: -min(d, NY - d))
    near_first = sorted(range(1, NX), key=lambda d: min(d, NX - d))
    def send_own(t):
        z_send(t).start()
        for d in near_first:
            x_send(t, 0, d).start()
        q_send(t, 0, 0).start()

    send_own(0)

    loads[4].wait()

    @pl.when(row > 0)
    def _():
        e_send().start()

    def init_send(t, d):
        there = pl.ds(((y + d) % NY) * CW, CW)
        return copy(
            init.at[t, there], carry_in.at[t], i_s.at[t], c_r.at[t], y_peer(d)
        )

    def send_init(t):
        for d in range(1, NY):
            init_send(t, d).start()
        carry_in[t] = init[t, pl.ds(0, CW)]

    @pl.when(row == 0)
    def _():
        init[0] = jnp.transpose(eig_ref[...])
        send_init(0)

    z_take(0)
    send_own(1)
    for d in near_first:
        x_take(0, 0, d)
    for d in near_first:
        x_take(0, 1, d)

    @pl.when(row < last_row)
    def _():
        arrived(below_raw, e_r)
        below[0] = jnp.transpose(below_raw[...])

    @pl.when(row == last_row)
    def _():
        below[0] = jnp.zeros((CL, NB), F32)

    q_take(0)

    UP, LOW, FAC = 0, 1, 2

    def parts(t, which):
        return ops_h[t, which], ops_l[t, which]

    def unpack(t):
        both = vf[t, :, :, :, pl.ds(0, RC), :].reshape(NB, NB)
        factor = vf[t, :, :, :, pl.ds(RC, RC), :].reshape(NB, NB)
        start = lax.broadcasted_iota(jnp.int32, (NB, NB), 0) + start_of(t)
        position = lax.broadcasted_iota(jnp.int32, (NB, NB), 1)
        zero = jnp.zeros_like(both)
        for which, value in (
            (UP, jnp.where(position >= start, both, zero)),
            (LOW, jnp.where(position < start, both, zero)),
            (FAC, factor),
        ):
            ops_h[t, which], ops_l[t, which] = split(value)

    def make_gain(t):
        inner = product(parts(t, FAC), parts(t, UP), NN)
        turned = split(jnp.transpose(inner))
        gain = -product(turned, parts(t, LOW), NN)
        gains[t, y, :, :HB] = gain[:HB, :HB] + jnp.transpose(gain[HB:, HB:])
        gains[t, y, :, HB:] = gain[HB:, :HB]
        return turned

    def spread_gain(t, i):
        square, corner = gains[t, i, :, :HB], gains[t, i, :, HB:]
        down = lax.broadcasted_iota(jnp.int32, (HB, HB), 0)
        across = lax.broadcasted_iota(jnp.int32, (HB, HB), 1)
        zero = jnp.zeros_like(square)
        first = jnp.where(down > across, square, zero)
        second = jnp.transpose(jnp.where(across > down, square, zero))
        for r, c, value in (
            (0, 0, first),
            (0, 1, zero),
            (1, 0, corner),
            (1, 1, second),
        ):
            high, low = split(value)
            gains_h[t, i, r * HB : (r + 1) * HB, c * HB : (c + 1) * HB] = high
            gains_l[t, i, r * HB : (r + 1) * HB, c * HB : (c + 1) * HB] = low

    def make_shift(t):
        rows = below[t]
        lowered = product(split(rows), parts(t, LOW), NT)
        proj[t] = lowered
        coeffs = split(product(split(lowered), parts(t, FAC), NT))
        d_out[t] = rows - product(coeffs, parts(t, LOW), NN)
        return coeffs

    def make_back(turned, coeffs):
        down = lax.broadcasted_iota(jnp.int32, (NB, NB), 0)
        across = lax.broadcasted_iota(jnp.int32, (NB, NB), 1)
        unit = jnp.where(down == across, 1.0, 0.0).astype(F32)
        back_out[...] = unit - product(turned, parts(0, UP), NN)
        rest_out[...] = -product(coeffs, parts(0, UP), NN)

    def finish(t, rows):
        coeffs = product(split(rows), parts(t, UP), NT) + proj[t]
        coeffs = product(split(coeffs), parts(t, FAC), NT)
        return rows - product(split(coeffs), parts(t, UP), NN)

    def share(column, core):
        at = core * SHARE + column * PART
        return pl.ds(pl.multiple_of(at, PART), PART)

    def half(core):
        return pl.ds(pl.multiple_of(core * SHARE, SHARE), SHARE)

    def source_of(d):
        return (y + NY - d) % NY

    def g_send(t, d):
        piece = gains.at[t, y, share(x, q)]
        return copy(piece, piece, g_s.at[t], g_r.at[t, d - 1], y_peer(d))

    def gx_send(t, d, way):
        piece = gains.at[t, source_of(d), share(x, q)]
        there = x_peer(1 if way == 0 else NX - 1)
        return copy(piece, piece, gx_s.at[t], gx_r.at[t, d - 1, way], there)

    def gx_from(way):
        return (x + NX - 1) % NX if way == 0 else (x + 1) % NX

    def gx_relay(t, d):
        way = d % 2
        piece = gains.at[t, source_of(d), share(gx_from(way), q)]
        there = x_peer(1 if way == 0 else NX - 1)
        return copy(piece, piece, gx_s.at[t], gx_r.at[t, d - 1, 2], there)

    def gq_send(t, d):
        piece = gains.at[t, source_of(d), half(q)]
        return copy(piece, piece, gq_s.at[t], gq_r.at[t, d - 1], sibling)

    def gain_start(t):
        for d in y_near_first:
            g_send(t, d).start()

    def gain_take(t, d):
        arrived(gains.at[t, source_of(d), share(x, q)], g_r.at[t, d - 1])
        for way in range(2):
            gx_send(t, d, way).start()

    def gain_relay(t, d):
        way = d % 2
        piece = gains.at[t, source_of(d), share(gx_from(way), q)]
        arrived(piece, gx_r.at[t, d - 1, way])
        gx_relay(t, d).start()

    def gain_pass(t, d):
        way = 1 - d % 2
        piece = gains.at[t, source_of(d), share(gx_from(way), q)]
        arrived(piece, gx_r.at[t, d - 1, way])
        far_piece = gains.at[t, source_of(d), share((x + 2) % NX, q)]
        arrived(far_piece, gx_r.at[t, d - 1, 2])
        gq_send(t, d).start()

    def gain_land(t, d):
        arrived(gains.at[t, source_of(d), half(1 - q)], gq_r.at[t, d - 1])
        spread_gain(t, source_of(d))

    def d_send(t, d):
        there = pl.ds(((y + d) % NY) * CW, CW)
        return copy(
            d_out.at[t, there], d_in.at[t, y], d_s.at[t], d_r.at[t], y_peer(d)
        )

    def send_shift(t):
        for d in y_far_first:
            d_send(t, d).start()
        d_in[t, y] = d_out[t, pl.ds(y * CW, CW)]

    def take_shift(t):
        arrived(d_in.at[t, pl.ds(0, NY - 1)], d_r.at[t])

    def owner_of(t, i):
        return i - 1 if t == 0 else i

    def state_send(t, i):
        return copy(
            states_out.at[t, i],
            states_in.at[t, pl.ds(y * CW, CW)],
            s_s.at[t],
            s_r.at[t],
            (k * NY + owner_of(t, i), col),
        )

    def share_state(t, i):
        if 0 <= owner_of(t, i) < NY:

            @pl.when(y != owner_of(t, i))
            def _():
                state_send(t, i).start()

    def carry_send(t):
        return copy(
            states_out.at[t, NY], carry_in.at[t], c_s.at[t], c_r.at[t], down_group
        )

    def chain(t):
        take_shift(t)

        @pl.when(row > 0)
        def _():
            arrived(carry_in.at[t], c_r.at[t])

        state = carry_in[t]
        for i in range(NY):
            states_out[t, i] = state
            share_state(t, i)
            high, low = split(state)
            gain_h = gains_h[t, i]
            pair = dot(jnp.concatenate([high, low], 0), gain_h, NN)
            state = (pair[:CW] + pair[CW:]) + (
                dot(high, gains_l[t, i], NN) + d_in[t, i]
            )
        states_out[t, NY] = state

        @pl.when(has_down)
        def _():
            carry_send(t).start()

        share_state(t, NY)

    def collect(t):
        mine = pl.ds(y * CW, CW)
        states_in[t, mine] = states_out[t, y + (1 - t)]
        arrived(states_in.at[t, pl.ds(0, (NY - 1) * CW)], s_r.at[t])

    def back_rows(column, core):
        at = (column * NQ + core) * BACK
        return pl.ds(pl.multiple_of(at, BACK), BACK)

    def a_send():
        rows = back_rows(x, q)
        return copy(back_out.at[rows], back_in.at[rows], a_s, a_r, up_row)

    def h_send():
        return copy(rest_out, rest_in, h_s, h_r, up_row)

    def ax_send(d):
        piece = back_in.at[back_rows(x, q)]
        return copy(piece, piece, ax_s, ax_r.at[d - 1], x_peer(d))

    def aq_send(d):
        piece = back_in.at[back_rows((x + NX - d) % NX, q)]
        return copy(piece, piece, aq_s, aq_r, sibling)

    def back_take():
        @pl.when(row < last_row)
        def _():
            arrived(back_in.at[back_rows(x, q)], a_r)
            for d in near_first:
                ax_send(d).start()
            aq_send(0).start()

    def back_pass():
        @pl.when(row < last_row)
        def _():
            for d in near_first:
                arrived(back_in.at[back_rows((x + NX - d) % NX, q)], ax_r.at[d - 1])
                aq_send(d).start()

    def back_land():
        arrived(back_in.at[pl.ds(0, NX * BACK)], aq_r)
        arrived(rest_in, h_r)

    def left(view, sem):
        copy(view, view, sem, z_r.at[0], sibling).wait_send()

    def left_early():
        for t in range(2):
            z_send(t).wait_send()
            left(vf.at[t, pl.ds(0, NX - 1), :, 0], x_s.at[t])
            left(vf.at[t, :, :, 0], q_s.at[t])

        @pl.when(row > 0)
        def _():
            e_send().wait_send()

    def left_ring(t):
        left(gains.at[t, pl.ds(0, NY - 1), pl.ds(0, PART)], g_s.at[t])
        left(gains.at[t, pl.ds(0, NY - 1), pl.ds(0, (NX - 1) * PART)], gx_s.at[t])
        left(gains.at[t, pl.ds(0, NY - 1), pl.ds(0, SHARE)], gq_s.at[t])
        left(d_out.at[t, pl.ds(0, (NY - 1) * CW)], d_s.at[t])

    def left_back():
        @pl.when(row > 0)
        def _():
            a_send().wait_send()
            h_send().wait_send()

        @pl.when(row < last_row)
        def _():
            left(back_in.at[pl.ds(0, (NX - 1) * BACK)], ax_s)
            left(back_in.at[pl.ds(0, NX * BACK)], aq_s)

        @pl.when(row == 0)
        def _():
            for t in range(2):
                left(init.at[t, pl.ds(0, (NY - 1) * CW)], i_s.at[t])

    def left_states(t):
        left(states_out.at[t, pl.ds(0, NY - 1)], s_s.at[t])

        @pl.when(has_down)
        def _():
            carry_send(t).wait_send()

    def each(step, t, ds):
        for d in ds:
            step(t, d)

    near, far = y_near_first[: NY // 2], y_near_first[NY // 2 :]
    unpack(0)
    turned = make_gain(0)
    gain_start(0)
    coeffs = make_shift(0)
    spread_gain(0, y)
    z_take(1)
    each(gain_take, 0, near)
    send_shift(0)
    make_back(turned, coeffs)

    @pl.when(row > 0)
    def _():
        a_send().start()
        h_send().start()

    each(gain_take, 0, far)
    each(gain_relay, 0, near)
    for p in range(2):
        for d in near_first:
            x_take(1, p, d)
    each(gain_relay, 0, far)
    each(gain_pass, 0, near)
    back_take()
    q_take(1)
    unpack(1)
    make_gain(1)
    gain_start(1)
    spread_gain(1, y)
    for d, e in zip(far, near):
        gain_pass(0, d)
        gain_land(0, e)
    for d in y_near_first[len(far) :]:
        gain_land(0, d)

    def bring():
        each(gain_take, 1, y_near_first)
        each(gain_relay, 1, near)

    def relay():
        each(gain_relay, 1, far)

    def hand():
        each(gain_pass, 1, y_near_first)

    def keep():
        each(gain_land, 1, y_near_first)

    @pl.when(k >= 1)
    def _():
        back_pass()

    @pl.when(k >= 2)
    def _():
        bring()
        relay()

    @pl.when(k >= 3)
    def _():
        hand()

    chain(0)

    @pl.when(k < 1)
    def _():
        back_pass()

    @pl.when(k < 2)
    def _():
        bring()

    @pl.when(k == 2)
    def _():
        hand()

    @pl.when(k >= 3)
    def _():
        keep()

    left_early()
    left_ring(0)
    collect(0)

    @pl.when(row < last_row)
    def _():
        back_land()
        below[1] = rest_in[...] + product(
            split(states_in[0]), split(back_in[...]), NN
        )

    @pl.when(row == last_row)
    def _():
        below[1] = jnp.zeros((CL, NB), F32)

    make_shift(1)
    send_shift(1)

    @pl.when(row == 0)
    def _():
        init[1] = finish(0, init[0])
        send_init(1)

    @pl.when(k < 2)
    def _():
        relay()
        hand()

    @pl.when(k < 3)
    def _():
        keep()

    chain(1)
    left_ring(1)
    left_states(0)
    left_back()
    collect(1)
    out_ref[...] = jnp.transpose(finish(1, states_in[1]))
    store = pltpu.make_async_copy(out_ref, out_hbm, own_s.at[3])
    store.start()
    left_states(1)
    store.wait()


def on_device(dims, eigvecs, reflectors, factors, offsets, sweep_order):
    KZ, NY, NX, NH, NQ = dims
    NB, CL = eigvecs.shape
    CW = CL // NY
    RC = reflectors.shape[2]
    DMA = pltpu.SemaphoreType.DMA
    hbm = pl.BlockSpec(memory_space=pltpu.HBM)
    return pl.pallas_call(
        functools.partial(kernel, dims),
        out_shape=jax.ShapeDtypeStruct((NB, CL), F32),
        in_specs=[hbm] * 5,
        out_specs=pl.BlockSpec(memory_space=pl.ANY),
        scratch_shapes=[
            pltpu.SMEM(sweep_order.shape, jnp.int32),
            pltpu.SMEM((offsets.shape[0],), jnp.int32),
            pltpu.VMEM(eigvecs.shape, F32),
            pltpu.VMEM(reflectors.shape, F32),
            pltpu.VMEM(factors.shape, F32),
            pltpu.VMEM(eigvecs.shape, F32),
            DMA((6,)),
            pltpu.VMEM((2, NX, NH, NQ, 2 * RC, NB), F32),
            pltpu.VMEM((2, 3, NB, NB), BF16),
            pltpu.VMEM((2, 3, NB, NB), BF16),
            pltpu.VMEM((2, CL, NB), F32),
            pltpu.VMEM((NB, CL), F32),
            pltpu.VMEM((2, CL, NB), F32),
            pltpu.VMEM((2, CL, NB), F32),
            pltpu.VMEM((2, NY, NB // 2, NB), F32),
            pltpu.VMEM((2, NY, NB, NB), BF16),
            pltpu.VMEM((2, NY, NB, NB), BF16),
            pltpu.VMEM((2, CL, NB), F32),
            pltpu.VMEM((2, NY, CW, NB), F32),
            pltpu.VMEM((2, CW, NB), F32),
            pltpu.VMEM((2, NY + 1, CW, NB), F32),
            pltpu.VMEM((2, CL, NB), F32),
            pltpu.VMEM((NB, NB), F32),
            pltpu.VMEM((NB, NB), F32),
            pltpu.VMEM((CL, NB), F32),
            pltpu.VMEM((CL, NB), F32),
            DMA((2,)),
            DMA((2,)),
            DMA((2,)),
            DMA((2, NH, NX)),
            DMA((2,)),
            DMA((2,)),
            DMA,
            DMA,
            DMA((2,)),
            DMA((2, NY - 1)),
            DMA((2,)),
            DMA((2, NY - 1, 3)),
            DMA((2,)),
            DMA((2, NY - 1)),
            DMA((2,)),
            DMA((2,)),
            DMA((2,)),
            DMA((2,)),
            DMA((2,)),
            DMA((2,)),
            DMA((2,)),
            DMA,
            DMA,
            DMA,
            DMA,
            DMA,
            DMA((NX - 1,)),
            DMA,
            DMA,
        ],
        compiler_params=pltpu.CompilerParams(
            collective_id=0, has_side_effects=True, vmem_limit_bytes=24 << 20
        ),
    )(
        *(
            pltpu.with_memory_space_constraint(part, pltpu.HBM)
            for part in (
                sweep_order,
                offsets.reshape(-1),
                eigvecs,
                reflectors,
                factors,
            )
        ),
    )


def build(mesh, dims):
    placed = (
        P("row", "col"),
        P(None, "row", "col", None),
        P(None, "row", "col", None),
        P(None, "row"),
        P(),
    )
    return jax.shard_map(
        functools.partial(on_device, dims),
        mesh=mesh,
        in_specs=placed,
        out_specs=P("row", "col"),
        check_vma=False,
    )


def solution(mesh):
    return build(mesh, (Z_LO, Y, X, Z_HI, CORES))
```

```python
import functools

import jax
import jax.numpy as jnp
from jax import lax
from jax.experimental import pallas as pl
from jax.experimental.pallas import tpu as pltpu
from jax.sharding import PartitionSpec as P

MESH = pl.DeviceIdType.MESH
F32, BF16 = jnp.float32, jnp.bfloat16
NN, NT = ((1,), (0,)), ((1,), (1,))

Z_LO, Y, X, Z_HI, CORES = 4, 8, 4, 2, 2


def split(value):
    high = value.astype(BF16)
    return high, (value - high.astype(F32)).astype(BF16)


def dot(left, right, dims):
    return lax.dot_general(left, right, (dims, ((), ())), preferred_element_type=F32)


def product(left, right, dims):
    (lh, ll), (rh, rl) = left, right
    return dot(lh, rh, dims) + (dot(lh, rl, dims) + dot(ll, rh, dims))


def kernel(
    dims,
    order_hbm,
    offs_hbm,
    eig_hbm,
    refl_hbm,
    fact_hbm,
    out_hbm,
    order_ref,
    offs_ref,
    eig_ref,
    refl_ref,
    fact_ref,
    out_ref,
    own_s,
    vf,
    ops_h,
    ops_l,
    proj,
    below_raw,
    below,
    init,
    gains,
    gains_h,
    gains_l,
    d_out,
    d_in,
    carry_in,
    states_out,
    states_in,
    whole_h,
    whole_l,
    fresh,
    back_out,
    back_in,
    rest_out,
    rest_in,
    z_s,
    z_r,
    x_s,
    x_r,
    q_s,
    q_r,
    e_s,
    e_r,
    g_s,
    g_r,
    gx_s,
    gx_r,
    gq_s,
    gq_r,
    d_s,
    d_r,
    i_s,
    c_s,
    c_r,
    s_s,
    s_r,
    a_s,
    a_r,
    h_s,
    h_r,
    ax_s,
    ax_r,
    aq_s,
    aq_r,
):
    KZ, NY, NX, NH, NQ = dims
    NB = eig_ref.shape[0]
    CL = eig_ref.shape[1]
    CW = CL // NY
    RC = refl_ref.shape[2]
    HB = NB // 2
    SHARE = HB // NQ
    PART = SHARE // NX
    BACK = NB // (NX * NQ)

    row, col = lax.axis_index("row"), lax.axis_index("col")
    k, y = row // NY, row % NY
    x, h, q = col // (NH * NQ), (col // NQ) % NH, col % NQ
    last_row = KZ * NY - 1

    def y_peer(d):
        return (k * NY + (y + d) % NY, col)

    def x_peer(d):
        return (row, ((x + d) % NX) * (NH * NQ) + h * NQ + q)

    z_peer = (row, x * (NH * NQ) + (1 - h) * NQ + q)
    sibling = (row, x * (NH * NQ) + h * NQ + (1 - q))
    up_group, down_group = (row - NY, col), (row + NY, col)
    up_row, down_row = (row - 1, col), (row + 1, col)

    def copy(src, dst, ssem, rsem, device):
        return pltpu.make_async_remote_copy(
            src_ref=src,
            dst_ref=dst,
            send_sem=ssem,
            recv_sem=rsem,
            device_id=device,
            device_id_type=MESH,
        )

    def arrived(dst, rsem):
        copy(dst, dst, z_s.at[0], rsem, sibling).wait_recv()

    loads = [
        pltpu.make_async_copy(order_hbm, order_ref, own_s.at[4]),
        pltpu.make_async_copy(offs_hbm, offs_ref, own_s.at[5]),
        pltpu.make_async_copy(refl_hbm, refl_ref, own_s.at[0]),
        pltpu.make_async_copy(fact_hbm, fact_ref, own_s.at[1]),
        pltpu.make_async_copy(eig_hbm, eig_ref, own_s.at[2]),
    ]
    for load in loads:
        load.start()

    barrier = pltpu.get_barrier_semaphore()

    def greet(device):
        pl.semaphore_signal(barrier, inc=1, device_id=device, device_id_type=MESH)

    greet(z_peer)
    greet(sibling)
    for d in range(1, NX):
        greet(x_peer(d))
    for d in range(1, NY):
        greet(y_peer(d))
    has_up, has_down = k > 0, k < KZ - 1
    first_y, final_y = y == 0, y == NY - 1

    @pl.when(has_up)
    def _():
        greet(up_group)

    @pl.when(has_down)
    def _():
        greet(down_group)

    @pl.when(has_up & first_y)
    def _():
        greet(up_row)

    @pl.when(has_down & final_y)
    def _():
        greet(down_row)

    for load in loads[:4]:
        load.wait()

    def start_of(t):
        return offs_ref[order_ref[t]]

    for t in range(2):
        chosen = order_ref[t]
        raw = refl_ref[chosen, 0]
        start = (
            col * RC + start_of(t) + lax.broadcasted_iota(jnp.int32, (RC, NB), 0)
        )
        position = lax.broadcasted_iota(jnp.int32, (RC, NB), 1)
        upper, lower = raw[:, :NB], raw[:, NB:]
        packed = jnp.where(position + NB >= start, lower, jnp.zeros_like(lower))
        packed = jnp.where(position >= start, upper, packed)
        unit = (position == start) | (position + NB == start)
        vf[t, x, h, q, pl.ds(0, RC)] = jnp.where(unit, jnp.ones_like(packed), packed)
        vf[t, x, h, q, pl.ds(RC, RC)] = fact_ref[chosen, 0]

    expected = (
        2
        + (NX - 1)
        + (NY - 1)
        + has_up.astype(jnp.int32)
        + has_down.astype(jnp.int32)
        + (has_up & first_y).astype(jnp.int32)
        + (has_down & final_y).astype(jnp.int32)
    )
    pl.semaphore_wait(barrier, expected)

    def z_send(t):
        piece = vf.at[t, x, h, q]
        return copy(piece, piece, z_s.at[t], z_r.at[t], z_peer)

    def x_send(t, p, d):
        piece = vf.at[t, x, h if p == 0 else 1 - h, q]
        return copy(piece, piece, x_s.at[t], x_r.at[t, p, d], x_peer(d))

    def q_send(t, p, d):
        piece = vf.at[t, (x + NX - d) % NX, h if p == 0 else 1 - h, q]
        return copy(piece, piece, q_s.at[t], q_r.at[t], sibling)

    def x_take(t, p, d):
        piece = vf.at[t, (x + NX - d) % NX, h if p == 0 else 1 - h, q]
        arrived(piece, x_r.at[t, p, d])
        q_send(t, p, d).start()

    def q_take(t):
        arrived(vf.at[t, :, :, 0], q_r.at[t])

    def z_take(t):
        arrived(vf.at[t, x, 1 - h, q], z_r.at[t])
        for d in range(1, NX):
            x_send(t, 1, d).start()
        q_send(t, 1, 0).start()

    def e_send():
        return copy(eig_ref, below_raw, e_s, e_r, up_row)

    y_near_first = sorted(range(1, NY), key=lambda d: min(d, NY - d))
    y_far_first = sorted(range(1, NY), key=lambda d: -min(d, NY - d))
    near_first = sorted(range(1, NX), key=lambda d: min(d, NX - d))
    def send_own(t):
        z_send(t).start()
        for d in near_first:
            x_send(t, 0, d).start()
        q_send(t, 0, 0).start()

    send_own(0)

    loads[4].wait()

    @pl.when(row > 0)
    def _():
        e_send().start()

    def init_send(t, d):
        there = pl.ds(((y + d) % NY) * CW, CW)
        return copy(
            init.at[t, there], carry_in.at[t], i_s.at[t], c_r.at[t], y_peer(d)
        )

    def send_init(t):
        for d in range(1, NY):
            init_send(t, d).start()
        carry_in[t] = init[t, pl.ds(0, CW)]

    @pl.when(row == 0)
    def _():
        init[0] = jnp.transpose(eig_ref[...])
        send_init(0)

    z_take(0)
    send_own(1)
    for d in near_first:
        x_take(0, 0, d)
    for d in near_first:
        x_take(0, 1, d)

    @pl.when(row < last_row)
    def _():
        arrived(below_raw, e_r)
        below[0] = jnp.transpose(below_raw[...])

    @pl.when(row == last_row)
    def _():
        below[0] = jnp.zeros((CL, NB), F32)

    q_take(0)

    UP, LOW, FAC = 0, 1, 2

    def parts(t, which):
        return ops_h[t, which], ops_l[t, which]

    def unpack(t):
        both = vf[t, :, :, :, pl.ds(0, RC), :].reshape(NB, NB)
        factor = vf[t, :, :, :, pl.ds(RC, RC), :].reshape(NB, NB)
        start = lax.broadcasted_iota(jnp.int32, (NB, NB), 0) + start_of(t)
        position = lax.broadcasted_iota(jnp.int32, (NB, NB), 1)
        zero = jnp.zeros_like(both)
        for which, value in (
            (UP, jnp.where(position >= start, both, zero)),
            (LOW, jnp.where(position < start, both, zero)),
            (FAC, factor),
        ):
            ops_h[t, which], ops_l[t, which] = split(value)

    def make_gain(t):
        inner = product(parts(t, FAC), parts(t, UP), NN)
        turned = split(jnp.transpose(inner))
        gain = -product(turned, parts(t, LOW), NN)
        gains[t, y, :, :HB] = gain[:HB, :HB] + jnp.transpose(gain[HB:, HB:])
        gains[t, y, :, HB:] = gain[HB:, :HB]
        return turned

    def spread_gain(t, i):
        square, corner = gains[t, i, :, :HB], gains[t, i, :, HB:]
        down = lax.broadcasted_iota(jnp.int32, (HB, HB), 0)
        across = lax.broadcasted_iota(jnp.int32, (HB, HB), 1)
        zero = jnp.zeros_like(square)
        first = jnp.where(down > across, square, zero)
        second = jnp.transpose(jnp.where(across > down, square, zero))
        for r, c, value in (
            (0, 0, first),
            (0, 1, zero),
            (1, 0, corner),
            (1, 1, second),
        ):
            high, low = split(value)
            gains_h[t, i, r * HB : (r + 1) * HB, c * HB : (c + 1) * HB] = high
            gains_l[t, i, r * HB : (r + 1) * HB, c * HB : (c + 1) * HB] = low

    def make_shift(t):
        rows = below[t]
        lowered = product(split(rows), parts(t, LOW), NT)
        proj[t] = lowered
        coeffs = split(product(split(lowered), parts(t, FAC), NT))
        d_out[t] = rows - product(coeffs, parts(t, LOW), NN)
        return coeffs

    def make_back(turned, coeffs):
        down = lax.broadcasted_iota(jnp.int32, (NB, NB), 0)
        across = lax.broadcasted_iota(jnp.int32, (NB, NB), 1)
        unit = jnp.where(down == across, 1.0, 0.0).astype(F32)
        back_out[...] = unit - product(turned, parts(0, UP), NN)
        rest_out[...] = -product(coeffs, parts(0, UP), NN)

    def finish(t, rows):
        coeffs = product(split(rows), parts(t, UP), NT) + proj[t]
        coeffs = product(split(coeffs), parts(t, FAC), NT)
        return rows - product(split(coeffs), parts(t, UP), NN)

    def share(column, core):
        at = core * SHARE + column * PART
        return pl.ds(pl.multiple_of(at, PART), PART)

    def half(core):
        return pl.ds(pl.multiple_of(core * SHARE, SHARE), SHARE)

    def source_of(d):
        return (y + NY - d) % NY

    def g_send(t, d):
        piece = gains.at[t, y, share(x, q)]
        return copy(piece, piece, g_s.at[t], g_r.at[t, d - 1], y_peer(d))

    def gx_send(t, d, way):
        piece = gains.at[t, source_of(d), share(x, q)]
        there = x_peer(1 if way == 0 else NX - 1)
        return copy(piece, piece, gx_s.at[t], gx_r.at[t, d - 1, way], there)

    def gx_from(way):
        return (x + NX - 1) % NX if way == 0 else (x + 1) % NX

    def gx_relay(t, d):
        way = d % 2
        piece = gains.at[t, source_of(d), share(gx_from(way), q)]
        there = x_peer(1 if way == 0 else NX - 1)
        return copy(piece, piece, gx_s.at[t], gx_r.at[t, d - 1, 2], there)

    def gq_send(t, d):
        piece = gains.at[t, source_of(d), half(q)]
        return copy(piece, piece, gq_s.at[t], gq_r.at[t, d - 1], sibling)

    def gain_start(t):
        for d in y_near_first:
            g_send(t, d).start()

    def gain_take(t, d):
        arrived(gains.at[t, source_of(d), share(x, q)], g_r.at[t, d - 1])
        for way in range(2):
            gx_send(t, d, way).start()

    def gain_relay(t, d):
        way = d % 2
        piece = gains.at[t, source_of(d), share(gx_from(way), q)]
        arrived(piece, gx_r.at[t, d - 1, way])
        gx_relay(t, d).start()

    def gain_pass(t, d):
        way = 1 - d % 2
        piece = gains.at[t, source_of(d), share(gx_from(way), q)]
        arrived(piece, gx_r.at[t, d - 1, way])
        far_piece = gains.at[t, source_of(d), share((x + 2) % NX, q)]
        arrived(far_piece, gx_r.at[t, d - 1, 2])
        gq_send(t, d).start()

    def gain_land(t, d):
        arrived(gains.at[t, source_of(d), half(1 - q)], gq_r.at[t, d - 1])
        spread_gain(t, source_of(d))

    def d_send(t, d):
        there = pl.ds(((y + d) % NY) * CW, CW)
        return copy(
            d_out.at[t, there], d_in.at[t, y], d_s.at[t], d_r.at[t], y_peer(d)
        )

    def send_shift(t):
        for d in y_far_first:
            d_send(t, d).start()
        d_in[t, y] = d_out[t, pl.ds(y * CW, CW)]

    def take_shift(t):
        arrived(d_in.at[t, pl.ds(0, NY - 1)], d_r.at[t])

    def owner_of(t, i):
        return i - 1 if t == 0 else i

    def state_send(t, i):
        return copy(
            states_out.at[t, i],
            states_in.at[t, pl.ds(y * CW, CW)],
            s_s.at[t],
            s_r.at[t],
            (k * NY + owner_of(t, i), col),
        )

    def share_state(t, i):
        if 0 <= owner_of(t, i) < NY:

            @pl.when(y != owner_of(t, i))
            def _():
                state_send(t, i).start()

    def carry_send(t):
        return copy(
            states_out.at[t, NY], carry_in.at[t], c_s.at[t], c_r.at[t], down_group
        )

    middle = has_up & has_down

    def step(t, i, state):
        high, low = split(state)
        pair = dot(jnp.concatenate([high, low], 0), gains_h[t, i], NN)
        return (pair[:CW] + pair[CW:]) + (dot(high, gains_l[t, i], NN) + d_in[t, i])

    def compose(t, with_fresh):
        whole_h[t], whole_l[t] = gains_h[t, 0], gains_l[t, 0]

        def join(i, state):
            longer = product(
                (whole_h[t], whole_l[t]), (gains_h[t, i], gains_l[t, i]), NN
            )
            if with_fresh:
                state = step(t, i, state)
            whole_h[t], whole_l[t] = split(longer)
            return state

        state = lax.fori_loop(1, NY, join, d_in[t, 0])
        if with_fresh:
            fresh[t] = state

    def chain(t):
        if t == 1:
            take_shift(t)

        @pl.when(middle)
        def _():
            if t == 1:
                state = d_in[t, 0]
                for i in range(1, NY):
                    state = step(t, i, state)
                fresh[t] = state
            arrived(carry_in.at[t], c_r.at[t])
            whole = whole_h[t], whole_l[t]
            states_out[t, NY] = product(split(carry_in[t]), whole, NN) + fresh[t]
            carry_send(t).start()
            share_state(t, NY)

        @pl.when((row > 0) & jnp.logical_not(middle))
        def _():
            arrived(carry_in.at[t], c_r.at[t])

        state = carry_in[t]
        for i in range(NY):
            states_out[t, i] = state
            share_state(t, i)
            state = step(t, i, state)

        @pl.when(jnp.logical_not(middle))
        def _():
            states_out[t, NY] = state

            @pl.when(has_down)
            def _():
                carry_send(t).start()

            share_state(t, NY)

    def collect(t):
        mine = pl.ds(y * CW, CW)
        states_in[t, mine] = states_out[t, y + (1 - t)]
        arrived(states_in.at[t, pl.ds(0, (NY - 1) * CW)], s_r.at[t])

    def back_rows(column, core):
        at = (column * NQ + core) * BACK
        return pl.ds(pl.multiple_of(at, BACK), BACK)

    def a_send():
        rows = back_rows(x, q)
        return copy(back_out.at[rows], back_in.at[rows], a_s, a_r, up_row)

    def h_send():
        return copy(rest_out, rest_in, h_s, h_r, up_row)

    def ax_send(d):
        piece = back_in.at[back_rows(x, q)]
        return copy(piece, piece, ax_s, ax_r.at[d - 1], x_peer(d))

    def aq_send(d):
        piece = back_in.at[back_rows((x + NX - d) % NX, q)]
        return copy(piece, piece, aq_s, aq_r, sibling)

    def back_take():
        @pl.when(row < last_row)
        def _():
            arrived(back_in.at[back_rows(x, q)], a_r)
            for d in near_first:
                ax_send(d).start()
            aq_send(0).start()

    def back_pass():
        @pl.when(row < last_row)
        def _():
            for d in near_first:
                arrived(back_in.at[back_rows((x + NX - d) % NX, q)], ax_r.at[d - 1])
                aq_send(d).start()

    def back_land():
        arrived(back_in.at[pl.ds(0, NX * BACK)], aq_r)
        arrived(rest_in, h_r)

    def left(view, sem):
        copy(view, view, sem, z_r.at[0], sibling).wait_send()

    def left_early():
        for t in range(2):
            z_send(t).wait_send()
            left(vf.at[t, pl.ds(0, NX - 1), :, 0], x_s.at[t])
            left(vf.at[t, :, :, 0], q_s.at[t])

        @pl.when(row > 0)
        def _():
            e_send().wait_send()

    def left_ring(t):
        left(gains.at[t, pl.ds(0, NY - 1), pl.ds(0, PART)], g_s.at[t])
        left(gains.at[t, pl.ds(0, NY - 1), pl.ds(0, (NX - 1) * PART)], gx_s.at[t])
        left(gains.at[t, pl.ds(0, NY - 1), pl.ds(0, SHARE)], gq_s.at[t])
        left(d_out.at[t, pl.ds(0, (NY - 1) * CW)], d_s.at[t])

    def left_back():
        @pl.when(row > 0)
        def _():
            a_send().wait_send()
            h_send().wait_send()

        @pl.when(row < last_row)
        def _():
            left(back_in.at[pl.ds(0, (NX - 1) * BACK)], ax_s)
            left(back_in.at[pl.ds(0, NX * BACK)], aq_s)

        @pl.when(row == 0)
        def _():
            for t in range(2):
                left(init.at[t, pl.ds(0, (NY - 1) * CW)], i_s.at[t])

    def left_states(t):
        left(states_out.at[t, pl.ds(0, NY - 1)], s_s.at[t])

        @pl.when(has_down)
        def _():
            carry_send(t).wait_send()

    def each(step, t, ds):
        for d in ds:
            step(t, d)

    near, far = y_near_first[: NY // 2], y_near_first[NY // 2 :]
    unpack(0)
    turned = make_gain(0)
    gain_start(0)
    coeffs = make_shift(0)
    spread_gain(0, y)
    z_take(1)
    each(gain_take, 0, near)
    send_shift(0)
    make_back(turned, coeffs)

    @pl.when(row > 0)
    def _():
        a_send().start()
        h_send().start()

    each(gain_take, 0, far)
    each(gain_relay, 0, near)
    for p in range(2):
        for d in near_first:
            x_take(1, p, d)
    each(gain_relay, 0, far)
    each(gain_pass, 0, near)
    back_take()
    q_take(1)
    unpack(1)
    make_gain(1)
    gain_start(1)
    spread_gain(1, y)
    for d, e in zip(far, near):
        gain_pass(0, d)
        gain_land(0, e)
    for d in y_near_first[len(far) :]:
        gain_land(0, d)

    def bring():
        each(gain_take, 1, y_near_first)

    def relay():
        each(gain_relay, 1, y_near_first)

    def hand():
        each(gain_pass, 1, y_near_first)

    def keep():
        each(gain_land, 1, y_near_first)

    @pl.when(k >= 1)
    def _():
        back_pass()

    @pl.when(middle)
    def _():
        take_shift(0)
        compose(0, True)

    @pl.when(k >= 2)
    def _():
        bring()

    @pl.when(k >= 3)
    def _():
        relay()

    @pl.when(jnp.logical_not(middle))
    def _():
        take_shift(0)

    chain(0)

    @pl.when(k < 1)
    def _():
        back_pass()

    @pl.when(k < 2)
    def _():
        bring()

    @pl.when((k == 1) | (k == 2))
    def _():
        relay()

    @pl.when(k >= 3)
    def _():
        hand()

    left_early()
    left_ring(0)
    collect(0)

    @pl.when(row < last_row)
    def _():
        back_land()
        below[1] = rest_in[...] + product(
            split(states_in[0]), split(back_in[...]), NN
        )

    @pl.when(row == last_row)
    def _():
        below[1] = jnp.zeros((CL, NB), F32)

    make_shift(1)
    send_shift(1)

    @pl.when(row == 0)
    def _():
        init[1] = finish(0, init[0])
        send_init(1)

    @pl.when(k < 1)
    def _():
        relay()

    @pl.when(k < 3)
    def _():
        hand()

    keep()

    @pl.when(middle)
    def _():
        compose(1, False)

    chain(1)
    left_ring(1)
    left_states(0)
    left_back()
    collect(1)
    out_ref[...] = jnp.transpose(finish(1, states_in[1]))
    store = pltpu.make_async_copy(out_ref, out_hbm, own_s.at[3])
    store.start()
    left_states(1)
    store.wait()


def on_device(dims, eigvecs, reflectors, factors, offsets, sweep_order):
    KZ, NY, NX, NH, NQ = dims
    NB, CL = eigvecs.shape
    CW = CL // NY
    RC = reflectors.shape[2]
    DMA = pltpu.SemaphoreType.DMA
    hbm = pl.BlockSpec(memory_space=pltpu.HBM)
    return pl.pallas_call(
        functools.partial(kernel, dims),
        out_shape=jax.ShapeDtypeStruct((NB, CL), F32),
        in_specs=[hbm] * 5,
        out_specs=pl.BlockSpec(memory_space=pl.ANY),
        scratch_shapes=[
            pltpu.SMEM(sweep_order.shape, jnp.int32),
            pltpu.SMEM((offsets.shape[0],), jnp.int32),
            pltpu.VMEM(eigvecs.shape, F32),
            pltpu.VMEM(reflectors.shape, F32),
            pltpu.VMEM(factors.shape, F32),
            pltpu.VMEM(eigvecs.shape, F32),
            DMA((6,)),
            pltpu.VMEM((2, NX, NH, NQ, 2 * RC, NB), F32),
            pltpu.VMEM((2, 3, NB, NB), BF16),
            pltpu.VMEM((2, 3, NB, NB), BF16),
            pltpu.VMEM((2, CL, NB), F32),
            pltpu.VMEM((NB, CL), F32),
            pltpu.VMEM((2, CL, NB), F32),
            pltpu.VMEM((2, CL, NB), F32),
            pltpu.VMEM((2, NY, NB // 2, NB), F32),
            pltpu.VMEM((2, NY, NB, NB), BF16),
            pltpu.VMEM((2, NY, NB, NB), BF16),
            pltpu.VMEM((2, CL, NB), F32),
            pltpu.VMEM((2, NY, CW, NB), F32),
            pltpu.VMEM((2, CW, NB), F32),
            pltpu.VMEM((2, NY + 1, CW, NB), F32),
            pltpu.VMEM((2, CL, NB), F32),
            pltpu.VMEM((2, NB, NB), BF16),
            pltpu.VMEM((2, NB, NB), BF16),
            pltpu.VMEM((2, CW, NB), F32),
            pltpu.VMEM((NB, NB), F32),
            pltpu.VMEM((NB, NB), F32),
            pltpu.VMEM((CL, NB), F32),
            pltpu.VMEM((CL, NB), F32),
            DMA((2,)),
            DMA((2,)),
            DMA((2,)),
            DMA((2, NH, NX)),
            DMA((2,)),
            DMA((2,)),
            DMA,
            DMA,
            DMA((2,)),
            DMA((2, NY - 1)),
            DMA((2,)),
            DMA((2, NY - 1, 3)),
            DMA((2,)),
            DMA((2, NY - 1)),
            DMA((2,)),
            DMA((2,)),
            DMA((2,)),
            DMA((2,)),
            DMA((2,)),
            DMA((2,)),
            DMA((2,)),
            DMA,
            DMA,
            DMA,
            DMA,
            DMA,
            DMA((NX - 1,)),
            DMA,
            DMA,
        ],
        compiler_params=pltpu.CompilerParams(
            collective_id=0, has_side_effects=True, vmem_limit_bytes=24 << 20
        ),
    )(
        *(
            pltpu.with_memory_space_constraint(part, pltpu.HBM)
            for part in (
                sweep_order,
                offsets.reshape(-1),
                eigvecs,
                reflectors,
                factors,
            )
        ),
    )


def build(mesh, dims):
    placed = (
        P("row", "col"),
        P(None, "row", "col", None),
        P(None, "row", "col", None),
        P(None, "row"),
        P(),
    )
    return jax.shard_map(
        functools.partial(on_device, dims),
        mesh=mesh,
        in_specs=placed,
        out_specs=P("row", "col"),
        check_vma=False,
    )


def solution(mesh):
    return build(mesh, (Z_LO, Y, X, Z_HI, CORES))
```

```python
import functools

import jax
import jax.numpy as jnp
from jax import lax
from jax.experimental import pallas as pl
from jax.experimental.pallas import tpu as pltpu
from jax.sharding import PartitionSpec as P

MESH = pl.DeviceIdType.MESH
F32, BF16 = jnp.float32, jnp.bfloat16
NN, NT = ((1,), (0,)), ((1,), (1,))

Z_LO, Y, X, Z_HI, CORES = 4, 8, 4, 2, 2


def split(value):
    high = value.astype(BF16)
    return high, (value - high.astype(F32)).astype(BF16)


def dot(left, right, dims):
    return lax.dot_general(left, right, (dims, ((), ())), preferred_element_type=F32)


def product(left, right, dims):
    (lh, ll), (rh, rl) = left, right
    return dot(lh, rh, dims) + (dot(lh, rl, dims) + dot(ll, rh, dims))


def kernel(
    dims,
    order_hbm,
    offs_hbm,
    eig_hbm,
    refl_hbm,
    fact_hbm,
    out_hbm,
    order_ref,
    offs_ref,
    eig_ref,
    refl_ref,
    fact_ref,
    out_ref,
    own_s,
    vf,
    ops_h,
    ops_l,
    proj,
    below_raw,
    below,
    init,
    gains,
    gains_h,
    gains_l,
    d_out,
    d_in,
    carry_in,
    states_out,
    states_in,
    whole_h,
    whole_l,
    fresh,
    back_out,
    back_in,
    rest_out,
    rest_in,
    z_s,
    z_r,
    x_s,
    x_r,
    q_s,
    q_r,
    e_s,
    e_r,
    g_s,
    g_r,
    gx_s,
    gx_r,
    gq_s,
    gq_r,
    d_s,
    d_r,
    i_s,
    c_s,
    c_r,
    s_s,
    s_r,
    a_s,
    a_r,
    h_s,
    h_r,
    ax_s,
    ax_r,
    aq_s,
    aq_r,
):
    KZ, NY, NX, NH, NQ = dims
    NB = eig_ref.shape[0]
    CL = eig_ref.shape[1]
    CW = CL // NY
    RC = refl_ref.shape[2]
    HB = NB // 2
    SHARE = HB // NQ
    PART = SHARE // NX
    BACK = NB // (NX * NQ)

    row, col = lax.axis_index("row"), lax.axis_index("col")
    k, y = row // NY, row % NY
    x, h, q = col // (NH * NQ), (col // NQ) % NH, col % NQ
    last_row = KZ * NY - 1

    def y_peer(d):
        return (k * NY + (y + d) % NY, col)

    def x_peer(d):
        return (row, ((x + d) % NX) * (NH * NQ) + h * NQ + q)

    z_peer = (row, x * (NH * NQ) + (1 - h) * NQ + q)
    sibling = (row, x * (NH * NQ) + h * NQ + (1 - q))
    up_group, down_group = (row - NY, col), (row + NY, col)
    up_row, down_row = (row - 1, col), (row + 1, col)

    def copy(src, dst, ssem, rsem, device):
        return pltpu.make_async_remote_copy(
            src_ref=src,
            dst_ref=dst,
            send_sem=ssem,
            recv_sem=rsem,
            device_id=device,
            device_id_type=MESH,
        )

    def arrived(dst, rsem):
        copy(dst, dst, z_s.at[0], rsem, sibling).wait_recv()

    loads = [
        pltpu.make_async_copy(order_hbm, order_ref, own_s.at[4]),
        pltpu.make_async_copy(offs_hbm, offs_ref, own_s.at[5]),
        pltpu.make_async_copy(refl_hbm, refl_ref, own_s.at[0]),
        pltpu.make_async_copy(fact_hbm, fact_ref, own_s.at[1]),
        pltpu.make_async_copy(eig_hbm, eig_ref, own_s.at[2]),
    ]
    for load in loads:
        load.start()

    barrier = pltpu.get_barrier_semaphore()

    def greet(device):
        pl.semaphore_signal(barrier, inc=1, device_id=device, device_id_type=MESH)

    greet(z_peer)
    greet(sibling)
    for d in range(1, NX):
        greet(x_peer(d))
    for d in range(1, NY):
        greet(y_peer(d))
    has_up, has_down = k > 0, k < KZ - 1
    first_y, final_y = y == 0, y == NY - 1

    @pl.when(has_up)
    def _():
        greet(up_group)

    @pl.when(has_down)
    def _():
        greet(down_group)

    @pl.when(has_up & first_y)
    def _():
        greet(up_row)

    @pl.when(has_down & final_y)
    def _():
        greet(down_row)

    for load in loads[:4]:
        load.wait()

    def start_of(t):
        return offs_ref[order_ref[t]]

    for t in range(2):
        chosen = order_ref[t]
        raw = refl_ref[chosen, 0]
        start = (
            col * RC + start_of(t) + lax.broadcasted_iota(jnp.int32, (RC, NB), 0)
        )
        position = lax.broadcasted_iota(jnp.int32, (RC, NB), 1)
        upper, lower = raw[:, :NB], raw[:, NB:]
        packed = jnp.where(position + NB >= start, lower, jnp.zeros_like(lower))
        packed = jnp.where(position >= start, upper, packed)
        unit = (position == start) | (position + NB == start)
        vf[t, x, h, q, pl.ds(0, RC)] = jnp.where(unit, jnp.ones_like(packed), packed)
        vf[t, x, h, q, pl.ds(RC, RC)] = fact_ref[chosen, 0]

    expected = (
        2
        + (NX - 1)
        + (NY - 1)
        + has_up.astype(jnp.int32)
        + has_down.astype(jnp.int32)
        + (has_up & first_y).astype(jnp.int32)
        + (has_down & final_y).astype(jnp.int32)
    )
    pl.semaphore_wait(barrier, expected)

    def z_send(t):
        piece = vf.at[t, x, h, q]
        return copy(piece, piece, z_s.at[t], z_r.at[t], z_peer)

    def x_send(t, p, d):
        piece = vf.at[t, x, h if p == 0 else 1 - h, q]
        return copy(piece, piece, x_s.at[t], x_r.at[t, p, d], x_peer(d))

    def q_send(t, p, d):
        piece = vf.at[t, (x + NX - d) % NX, h if p == 0 else 1 - h, q]
        return copy(piece, piece, q_s.at[t], q_r.at[t], sibling)

    def x_take(t, p, d):
        piece = vf.at[t, (x + NX - d) % NX, h if p == 0 else 1 - h, q]
        arrived(piece, x_r.at[t, p, d])
        q_send(t, p, d).start()

    def q_take(t):
        arrived(vf.at[t, :, :, 0], q_r.at[t])

    def z_take(t):
        arrived(vf.at[t, x, 1 - h, q], z_r.at[t])
        for d in range(1, NX):
            x_send(t, 1, d).start()
        q_send(t, 1, 0).start()

    def e_send():
        return copy(eig_ref, below_raw, e_s, e_r, up_row)

    y_near_first = sorted(range(1, NY), key=lambda d: min(d, NY - d))
    y_far_first = sorted(range(1, NY), key=lambda d: -min(d, NY - d))
    near_first = sorted(range(1, NX), key=lambda d: min(d, NX - d))
    def send_own(t):
        z_send(t).start()
        for d in near_first:
            x_send(t, 0, d).start()
        q_send(t, 0, 0).start()

    send_own(0)

    loads[4].wait()

    @pl.when(row > 0)
    def _():
        e_send().start()

    def init_send(t, d):
        there = pl.ds(((y + d) % NY) * CW, CW)
        return copy(
            init.at[t, there], carry_in.at[t], i_s.at[t], c_r.at[t], y_peer(d)
        )

    def send_init(t):
        for d in range(1, NY):
            init_send(t, d).start()
        carry_in[t] = init[t, pl.ds(0, CW)]

    @pl.when(row == 0)
    def _():
        init[0] = jnp.transpose(eig_ref[...])
        send_init(0)

    z_take(0)
    send_own(1)
    for d in near_first:
        x_take(0, 0, d)
    for d in near_first:
        x_take(0, 1, d)

    @pl.when(row < last_row)
    def _():
        arrived(below_raw, e_r)
        below[0] = jnp.transpose(below_raw[...])

    @pl.when(row == last_row)
    def _():
        below[0] = jnp.zeros((CL, NB), F32)

    q_take(0)

    UP, LOW, FAC = 0, 1, 2

    def parts(t, which):
        return ops_h[t, which], ops_l[t, which]

    def unpack(t):
        both = vf[t, :, :, :, pl.ds(0, RC), :].reshape(NB, NB)
        factor = vf[t, :, :, :, pl.ds(RC, RC), :].reshape(NB, NB)
        start = lax.broadcasted_iota(jnp.int32, (NB, NB), 0) + start_of(t)
        position = lax.broadcasted_iota(jnp.int32, (NB, NB), 1)
        zero = jnp.zeros_like(both)
        for which, value in (
            (UP, jnp.where(position >= start, both, zero)),
            (LOW, jnp.where(position < start, both, zero)),
            (FAC, factor),
        ):
            ops_h[t, which], ops_l[t, which] = split(value)

    def make_gain(t):
        inner = product(parts(t, FAC), parts(t, UP), NN)
        turned = split(jnp.transpose(inner))
        gain = -product(turned, parts(t, LOW), NN)
        gains[t, y, :, :HB] = gain[:HB, :HB] + jnp.transpose(gain[HB:, HB:])
        gains[t, y, :, HB:] = gain[HB:, :HB]
        return turned

    def spread_gain(t, i):
        square, corner = gains[t, i, :, :HB], gains[t, i, :, HB:]
        down = lax.broadcasted_iota(jnp.int32, (HB, HB), 0)
        across = lax.broadcasted_iota(jnp.int32, (HB, HB), 1)
        zero = jnp.zeros_like(square)
        first = jnp.where(down > across, square, zero)
        second = jnp.transpose(jnp.where(across > down, square, zero))
        for r, c, value in (
            (0, 0, first),
            (0, 1, zero),
            (1, 0, corner),
            (1, 1, second),
        ):
            high, low = split(value)
            gains_h[t, i, r * HB : (r + 1) * HB, c * HB : (c + 1) * HB] = high
            gains_l[t, i, r * HB : (r + 1) * HB, c * HB : (c + 1) * HB] = low

    def make_shift(t):
        rows = below[t]
        lowered = product(split(rows), parts(t, LOW), NT)
        proj[t] = lowered
        coeffs = split(product(split(lowered), parts(t, FAC), NT))
        d_out[t] = rows - product(coeffs, parts(t, LOW), NN)
        return coeffs

    def make_back(turned, coeffs):
        down = lax.broadcasted_iota(jnp.int32, (NB, NB), 0)
        across = lax.broadcasted_iota(jnp.int32, (NB, NB), 1)
        unit = jnp.where(down == across, 1.0, 0.0).astype(F32)
        back_out[...] = unit - product(turned, parts(0, UP), NN)
        rest_out[...] = -product(coeffs, parts(0, UP), NN)

    def finish(t, rows):
        coeffs = product(split(rows), parts(t, UP), NT) + proj[t]
        coeffs = product(split(coeffs), parts(t, FAC), NT)
        return rows - product(split(coeffs), parts(t, UP), NN)

    def share(column, core):
        at = core * SHARE + column * PART
        return pl.ds(pl.multiple_of(at, PART), PART)

    def half(core):
        return pl.ds(pl.multiple_of(core * SHARE, SHARE), SHARE)

    def source_of(d):
        return (y + NY - d) % NY

    def g_send(t, d):
        piece = gains.at[t, y, share(x, q)]
        return copy(piece, piece, g_s.at[t], g_r.at[t, d - 1], y_peer(d))

    def gx_send(t, d, e):
        piece = gains.at[t, source_of(d), share(x, q)]
        return copy(piece, piece, gx_s.at[t], gx_r.at[t, d - 1], x_peer(e))

    def gq_send(t, d):
        piece = gains.at[t, source_of(d), half(q)]
        return copy(piece, piece, gq_s.at[t], gq_r.at[t, d - 1], sibling)

    def gain_start(t):
        for d in y_near_first:
            g_send(t, d).start()

    def gain_take(t, d):
        arrived(gains.at[t, source_of(d), share(x, q)], g_r.at[t, d - 1])
        for e in near_first:
            gx_send(t, d, e).start()

    def gain_pass(t, d):
        arrived(gains.at[t, 0, pl.ds(0, (NX - 1) * PART)], gx_r.at[t, d - 1])
        gq_send(t, d).start()

    def gain_land(t, d):
        arrived(gains.at[t, source_of(d), half(1 - q)], gq_r.at[t, d - 1])
        spread_gain(t, source_of(d))

    def d_send(t, d):
        there = pl.ds(((y + d) % NY) * CW, CW)
        return copy(
            d_out.at[t, there], d_in.at[t, y], d_s.at[t], d_r.at[t], y_peer(d)
        )

    def send_shift(t):
        for d in y_far_first:
            d_send(t, d).start()
        d_in[t, y] = d_out[t, pl.ds(y * CW, CW)]

    def take_shift(t):
        arrived(d_in.at[t, pl.ds(0, NY - 1)], d_r.at[t])

    def owner_of(t, i):
        return i - 1 if t == 0 else i

    def state_send(t, i):
        return copy(
            states_out.at[t, i],
            states_in.at[t, pl.ds(y * CW, CW)],
            s_s.at[t],
            s_r.at[t],
            (k * NY + owner_of(t, i), col),
        )

    def share_state(t, i):
        if 0 <= owner_of(t, i) < NY:

            @pl.when(y != owner_of(t, i))
            def _():
                state_send(t, i).start()

    def carry_send(t):
        return copy(
            states_out.at[t, NY], carry_in.at[t], c_s.at[t], c_r.at[t], down_group
        )

    middle = has_up & has_down

    def step(t, i, state):
        high, low = split(state)
        pair = dot(jnp.concatenate([high, low], 0), gains_h[t, i], NN)
        return (pair[:CW] + pair[CW:]) + (dot(high, gains_l[t, i], NN) + d_in[t, i])

    def compose(t, with_fresh):
        whole_h[t], whole_l[t] = gains_h[t, 0], gains_l[t, 0]

        def join(i, state):
            longer = product(
                (whole_h[t], whole_l[t]), (gains_h[t, i], gains_l[t, i]), NN
            )
            if with_fresh:
                state = step(t, i, state)
            whole_h[t], whole_l[t] = split(longer)
            return state

        state = lax.fori_loop(1, NY, join, d_in[t, 0])
        if with_fresh:
            fresh[t] = state

    def chain(t):
        if t == 1:
            take_shift(t)

        @pl.when(middle)
        def _():
            if t == 1:
                state = d_in[t, 0]
                for i in range(1, NY):
                    state = step(t, i, state)
                fresh[t] = state
            arrived(carry_in.at[t], c_r.at[t])
            whole = whole_h[t], whole_l[t]
            states_out[t, NY] = product(split(carry_in[t]), whole, NN) + fresh[t]
            carry_send(t).start()
            share_state(t, NY)

        @pl.when((row > 0) & jnp.logical_not(middle))
        def _():
            arrived(carry_in.at[t], c_r.at[t])

        state = carry_in[t]
        for i in range(NY):
            states_out[t, i] = state
            share_state(t, i)
            state = step(t, i, state)

        @pl.when(jnp.logical_not(middle))
        def _():
            states_out[t, NY] = state

            @pl.when(has_down)
            def _():
                carry_send(t).start()

            share_state(t, NY)

    def collect(t):
        mine = pl.ds(y * CW, CW)
        states_in[t, mine] = states_out[t, y + (1 - t)]
        arrived(states_in.at[t, pl.ds(0, (NY - 1) * CW)], s_r.at[t])

    def back_rows(column, core):
        at = (column * NQ + core) * BACK
        return pl.ds(pl.multiple_of(at, BACK), BACK)

    def a_send():
        rows = back_rows(x, q)
        return copy(back_out.at[rows], back_in.at[rows], a_s, a_r, up_row)

    def h_send():
        return copy(rest_out, rest_in, h_s, h_r, up_row)

    def ax_send(d):
        piece = back_in.at[back_rows(x, q)]
        return copy(piece, piece, ax_s, ax_r.at[d - 1], x_peer(d))

    def aq_send(d):
        piece = back_in.at[back_rows((x + NX - d) % NX, q)]
        return copy(piece, piece, aq_s, aq_r, sibling)

    def back_take():
        @pl.when(row < last_row)
        def _():
            arrived(back_in.at[back_rows(x, q)], a_r)
            for d in near_first:
                ax_send(d).start()
            aq_send(0).start()

    def back_pass():
        @pl.when(row < last_row)
        def _():
            for d in near_first:
                arrived(back_in.at[back_rows((x + NX - d) % NX, q)], ax_r.at[d - 1])
                aq_send(d).start()

    def back_land():
        arrived(back_in.at[pl.ds(0, NX * BACK)], aq_r)
        arrived(rest_in, h_r)

    def left(view, sem):
        copy(view, view, sem, z_r.at[0], sibling).wait_send()

    def left_early():
        for t in range(2):
            z_send(t).wait_send()
            left(vf.at[t, pl.ds(0, NX - 1), :, 0], x_s.at[t])
            left(vf.at[t, :, :, 0], q_s.at[t])

        @pl.when(row > 0)
        def _():
            e_send().wait_send()

    def left_ring(t):
        left(gains.at[t, pl.ds(0, NY - 1), pl.ds(0, PART)], g_s.at[t])
        left(gains.at[t, pl.ds(0, NY - 1), pl.ds(0, (NX - 1) * PART)], gx_s.at[t])
        left(gains.at[t, pl.ds(0, NY - 1), pl.ds(0, SHARE)], gq_s.at[t])
        left(d_out.at[t, pl.ds(0, (NY - 1) * CW)], d_s.at[t])

    def left_back():
        @pl.when(row > 0)
        def _():
            a_send().wait_send()
            h_send().wait_send()

        @pl.when(row < last_row)
        def _():
            left(back_in.at[pl.ds(0, (NX - 1) * BACK)], ax_s)
            left(back_in.at[pl.ds(0, NX * BACK)], aq_s)

        @pl.when(row == 0)
        def _():
            for t in range(2):
                left(init.at[t, pl.ds(0, (NY - 1) * CW)], i_s.at[t])

    def left_states(t):
        left(states_out.at[t, pl.ds(0, NY - 1)], s_s.at[t])

        @pl.when(has_down)
        def _():
            carry_send(t).wait_send()

    def each(step, t, ds):
        for d in ds:
            step(t, d)

    near, far = y_near_first[: NY // 2], y_near_first[NY // 2 :]
    unpack(0)
    turned = make_gain(0)
    gain_start(0)
    coeffs = make_shift(0)
    spread_gain(0, y)
    z_take(1)
    each(gain_take, 0, near)
    send_shift(0)
    make_back(turned, coeffs)

    @pl.when(row > 0)
    def _():
        a_send().start()
        h_send().start()

    each(gain_take, 0, far)
    for p in range(2):
        for d in near_first:
            x_take(1, p, d)
    q_take(1)
    unpack(1)
    make_gain(1)
    gain_start(1)
    spread_gain(1, y)
    each(gain_pass, 0, near)
    back_take()
    for d, e in zip(far, near):
        gain_pass(0, d)
        gain_land(0, e)
    for d in y_near_first[len(far) :]:
        gain_land(0, d)

    def bring():
        each(gain_take, 1, y_near_first)

    def hand():
        each(gain_pass, 1, y_near_first)

    def keep():
        each(gain_land, 1, y_near_first)

    @pl.when(k >= 1)
    def _():
        back_pass()

    @pl.when(middle)
    def _():
        take_shift(0)
        compose(0, True)

    @pl.when(k >= 2)
    def _():
        bring()

    @pl.when(jnp.logical_not(middle))
    def _():
        take_shift(0)

    chain(0)

    @pl.when(k < 1)
    def _():
        back_pass()

    @pl.when(k < 2)
    def _():
        bring()

    @pl.when(k >= 2)
    def _():
        hand()

    left_early()
    left_ring(0)
    collect(0)

    @pl.when(row < last_row)
    def _():
        back_land()
        below[1] = rest_in[...] + product(
            split(states_in[0]), split(back_in[...]), NN
        )

    @pl.when(row == last_row)
    def _():
        below[1] = jnp.zeros((CL, NB), F32)

    make_shift(1)
    send_shift(1)

    @pl.when(row == 0)
    def _():
        init[1] = finish(0, init[0])
        send_init(1)

    @pl.when(k < 2)
    def _():
        hand()

    keep()

    @pl.when(middle)
    def _():
        compose(1, False)

    chain(1)
    left_ring(1)
    left_states(0)
    left_back()
    collect(1)
    out_ref[...] = jnp.transpose(finish(1, states_in[1]))
    store = pltpu.make_async_copy(out_ref, out_hbm, own_s.at[3])
    store.start()
    left_states(1)
    store.wait()


def on_device(dims, eigvecs, reflectors, factors, offsets, sweep_order):
    KZ, NY, NX, NH, NQ = dims
    NB, CL = eigvecs.shape
    CW = CL // NY
    RC = reflectors.shape[2]
    DMA = pltpu.SemaphoreType.DMA
    hbm = pl.BlockSpec(memory_space=pltpu.HBM)
    return pl.pallas_call(
        functools.partial(kernel, dims),
        out_shape=jax.ShapeDtypeStruct((NB, CL), F32),
        in_specs=[hbm] * 5,
        out_specs=pl.BlockSpec(memory_space=pl.ANY),
        scratch_shapes=[
            pltpu.SMEM(sweep_order.shape, jnp.int32),
            pltpu.SMEM((offsets.shape[0],), jnp.int32),
            pltpu.VMEM(eigvecs.shape, F32),
            pltpu.VMEM(reflectors.shape, F32),
            pltpu.VMEM(factors.shape, F32),
            pltpu.VMEM(eigvecs.shape, F32),
            DMA((6,)),
            pltpu.VMEM((2, NX, NH, NQ, 2 * RC, NB), F32),
            pltpu.VMEM((2, 3, NB, NB), BF16),
            pltpu.VMEM((2, 3, NB, NB), BF16),
            pltpu.VMEM((2, CL, NB), F32),
            pltpu.VMEM((NB, CL), F32),
            pltpu.VMEM((2, CL, NB), F32),
            pltpu.VMEM((2, CL, NB), F32),
            pltpu.VMEM((2, NY, NB // 2, NB), F32),
            pltpu.VMEM((2, NY, NB, NB), BF16),
            pltpu.VMEM((2, NY, NB, NB), BF16),
            pltpu.VMEM((2, CL, NB), F32),
            pltpu.VMEM((2, NY, CW, NB), F32),
            pltpu.VMEM((2, CW, NB), F32),
            pltpu.VMEM((2, NY + 1, CW, NB), F32),
            pltpu.VMEM((2, CL, NB), F32),
            pltpu.VMEM((2, NB, NB), BF16),
            pltpu.VMEM((2, NB, NB), BF16),
            pltpu.VMEM((2, CW, NB), F32),
            pltpu.VMEM((NB, NB), F32),
            pltpu.VMEM((NB, NB), F32),
            pltpu.VMEM((CL, NB), F32),
            pltpu.VMEM((CL, NB), F32),
            DMA((2,)),
            DMA((2,)),
            DMA((2,)),
            DMA((2, NH, NX)),
            DMA((2,)),
            DMA((2,)),
            DMA,
            DMA,
            DMA((2,)),
            DMA((2, NY - 1)),
            DMA((2,)),
            DMA((2, NY - 1)),
            DMA((2,)),
            DMA((2, NY - 1)),
            DMA((2,)),
            DMA((2,)),
            DMA((2,)),
            DMA((2,)),
            DMA((2,)),
            DMA((2,)),
            DMA((2,)),
            DMA,
            DMA,
            DMA,
            DMA,
            DMA,
            DMA((NX - 1,)),
            DMA,
            DMA,
        ],
        compiler_params=pltpu.CompilerParams(
            collective_id=0, has_side_effects=True, vmem_limit_bytes=24 << 20
        ),
    )(
        *(
            pltpu.with_memory_space_constraint(part, pltpu.HBM)
            for part in (
                sweep_order,
                offsets.reshape(-1),
                eigvecs,
                reflectors,
                factors,
            )
        ),
    )


def build(mesh, dims):
    placed = (
        P("row", "col"),
        P(None, "row", "col", None),
        P(None, "row", "col", None),
        P(None, "row"),
        P(),
    )
    return jax.shard_map(
        functools.partial(on_device, dims),
        mesh=mesh,
        in_specs=placed,
        out_specs=P("row", "col"),
        check_vma=False,
    )


def solution(mesh):
    return build(mesh, (Z_LO, Y, X, Z_HI, CORES))
```

```python
import functools

import jax
import jax.numpy as jnp
from jax import lax
from jax.experimental import pallas as pl
from jax.experimental.pallas import tpu as pltpu
from jax.sharding import PartitionSpec as P

MESH = pl.DeviceIdType.MESH
F32, BF16 = jnp.float32, jnp.bfloat16
NN, NT = ((1,), (0,)), ((1,), (1,))

Z_LO, Y, X, Z_HI, CORES = 4, 8, 4, 2, 2


def split(value):
    high = value.astype(BF16)
    return high, (value - high.astype(F32)).astype(BF16)


def dot(left, right, dims):
    return lax.dot_general(left, right, (dims, ((), ())), preferred_element_type=F32)


def product(left, right, dims):
    (lh, ll), (rh, rl) = left, right
    return dot(lh, rh, dims) + (dot(lh, rl, dims) + dot(ll, rh, dims))


def kernel(
    dims,
    order_hbm,
    offs_hbm,
    eig_hbm,
    refl_hbm,
    fact_hbm,
    out_hbm,
    order_ref,
    offs_ref,
    eig_ref,
    refl_ref,
    fact_ref,
    out_ref,
    own_s,
    vf,
    ops_h,
    ops_l,
    proj,
    below_raw,
    below,
    init,
    gains,
    gains_h,
    gains_l,
    d_out,
    d_in,
    carry_in,
    states_out,
    states_in,
    whole_h,
    whole_l,
    fresh,
    back_out,
    back_in,
    rest_out,
    rest_in,
    z_s,
    z_r,
    x_s,
    x_r,
    q_s,
    q_r,
    e_s,
    e_r,
    g_s,
    g_r,
    gx_s,
    gx_r,
    gq_s,
    gq_r,
    d_s,
    d_r,
    i_s,
    c_s,
    c_r,
    s_s,
    s_r,
    a_s,
    a_r,
    h_s,
    h_r,
    ax_s,
    ax_r,
    aq_s,
    aq_r,
):
    KZ, NY, NX, NH, NQ = dims
    NB = eig_ref.shape[0]
    CL = eig_ref.shape[1]
    CW = CL // NY
    RC = refl_ref.shape[2]
    HB = NB // 2
    SHARE = HB // NQ
    PART = SHARE // NX
    BACK = NB // (NX * NQ)

    row, col = lax.axis_index("row"), lax.axis_index("col")
    k, y = row // NY, row % NY
    x, h, q = col // (NH * NQ), (col // NQ) % NH, col % NQ
    last_row = KZ * NY - 1

    def y_peer(d):
        return (k * NY + (y + d) % NY, col)

    def x_peer(d):
        return (row, ((x + d) % NX) * (NH * NQ) + h * NQ + q)

    z_peer = (row, x * (NH * NQ) + (1 - h) * NQ + q)
    sibling = (row, x * (NH * NQ) + h * NQ + (1 - q))
    up_group, down_group = (row - NY, col), (row + NY, col)
    up_row, down_row = (row - 1, col), (row + 1, col)

    def copy(src, dst, ssem, rsem, device):
        return pltpu.make_async_remote_copy(
            src_ref=src,
            dst_ref=dst,
            send_sem=ssem,
            recv_sem=rsem,
            device_id=device,
            device_id_type=MESH,
        )

    def arrived(dst, rsem):
        copy(dst, dst, z_s.at[0], rsem, sibling).wait_recv()

    loads = [
        pltpu.make_async_copy(order_hbm, order_ref, own_s.at[4]),
        pltpu.make_async_copy(offs_hbm, offs_ref, own_s.at[5]),
        pltpu.make_async_copy(refl_hbm, refl_ref, own_s.at[0]),
        pltpu.make_async_copy(fact_hbm, fact_ref, own_s.at[1]),
        pltpu.make_async_copy(eig_hbm, eig_ref, own_s.at[2]),
    ]
    for load in loads:
        load.start()

    barrier = pltpu.get_barrier_semaphore()

    def greet(device):
        pl.semaphore_signal(barrier, inc=1, device_id=device, device_id_type=MESH)

    greet(z_peer)
    greet(sibling)
    for d in range(1, NX):
        greet(x_peer(d))
    for d in range(1, NY):
        greet(y_peer(d))
    has_up, has_down = k > 0, k < KZ - 1
    first_y, final_y = y == 0, y == NY - 1

    @pl.when(has_up)
    def _():
        greet(up_group)

    @pl.when(has_down)
    def _():
        greet(down_group)

    @pl.when(has_up & first_y)
    def _():
        greet(up_row)

    @pl.when(has_down & final_y)
    def _():
        greet(down_row)

    for load in loads[:4]:
        load.wait()

    def start_of(t):
        return offs_ref[order_ref[t]]

    for t in range(2):
        chosen = order_ref[t]
        raw = refl_ref[chosen, 0]
        start = (
            col * RC + start_of(t) + lax.broadcasted_iota(jnp.int32, (RC, NB), 0)
        )
        position = lax.broadcasted_iota(jnp.int32, (RC, NB), 1)
        upper, lower = raw[:, :NB], raw[:, NB:]
        packed = jnp.where(position + NB >= start, lower, jnp.zeros_like(lower))
        packed = jnp.where(position >= start, upper, packed)
        unit = (position == start) | (position + NB == start)
        vf[t, x, h, q, pl.ds(0, RC)] = jnp.where(unit, jnp.ones_like(packed), packed)
        vf[t, x, h, q, pl.ds(RC, RC)] = fact_ref[chosen, 0]

    expected = (
        2
        + (NX - 1)
        + (NY - 1)
        + has_up.astype(jnp.int32)
        + has_down.astype(jnp.int32)
        + (has_up & first_y).astype(jnp.int32)
        + (has_down & final_y).astype(jnp.int32)
    )
    pl.semaphore_wait(barrier, expected)

    def z_send(t):
        piece = vf.at[t, x, h, q]
        return copy(piece, piece, z_s.at[t], z_r.at[t], z_peer)

    def x_send(t, p, d):
        piece = vf.at[t, x, h if p == 0 else 1 - h, q]
        return copy(piece, piece, x_s.at[t], x_r.at[t, p, d], x_peer(d))

    def q_send(t, p, d):
        piece = vf.at[t, (x + NX - d) % NX, h if p == 0 else 1 - h, q]
        return copy(piece, piece, q_s.at[t], q_r.at[t], sibling)

    def x_take(t, p, d):
        piece = vf.at[t, (x + NX - d) % NX, h if p == 0 else 1 - h, q]
        arrived(piece, x_r.at[t, p, d])
        q_send(t, p, d).start()

    def q_take(t):
        arrived(vf.at[t, :, :, 0], q_r.at[t])

    def z_take(t):
        arrived(vf.at[t, x, 1 - h, q], z_r.at[t])
        for d in range(1, NX):
            x_send(t, 1, d).start()
        q_send(t, 1, 0).start()

    def e_send():
        return copy(eig_ref, below_raw, e_s, e_r, up_row)

    y_near_first = sorted(range(1, NY), key=lambda d: min(d, NY - d))
    y_far_first = sorted(range(1, NY), key=lambda d: -min(d, NY - d))
    near_first = sorted(range(1, NX), key=lambda d: min(d, NX - d))
    def send_own(t):
        z_send(t).start()
        for d in near_first:
            x_send(t, 0, d).start()
        q_send(t, 0, 0).start()

    send_own(0)

    loads[4].wait()

    @pl.when(row > 0)
    def _():
        e_send().start()

    def init_send(t, d):
        there = pl.ds(((y + d) % NY) * CW, CW)
        return copy(
            init.at[t, there], carry_in.at[t], i_s.at[t], c_r.at[t], y_peer(d)
        )

    def send_init(t):
        for d in range(1, NY):
            init_send(t, d).start()
        carry_in[t] = init[t, pl.ds(0, CW)]

    @pl.when(row == 0)
    def _():
        init[0] = jnp.transpose(eig_ref[...])
        send_init(0)

    z_take(0)
    send_own(1)
    for d in near_first:
        x_take(0, 0, d)
    for d in near_first:
        x_take(0, 1, d)

    @pl.when(row < last_row)
    def _():
        arrived(below_raw, e_r)
        below[0] = jnp.transpose(below_raw[...])

    @pl.when(row == last_row)
    def _():
        below[0] = jnp.zeros((CL, NB), F32)

    q_take(0)

    UP, LOW, FAC = 0, 1, 2

    def parts(t, which):
        return ops_h[t, which], ops_l[t, which]

    def unpack(t):
        both = vf[t, :, :, :, pl.ds(0, RC), :].reshape(NB, NB)
        factor = vf[t, :, :, :, pl.ds(RC, RC), :].reshape(NB, NB)
        start = lax.broadcasted_iota(jnp.int32, (NB, NB), 0) + start_of(t)
        position = lax.broadcasted_iota(jnp.int32, (NB, NB), 1)
        zero = jnp.zeros_like(both)
        for which, value in (
            (UP, jnp.where(position >= start, both, zero)),
            (LOW, jnp.where(position < start, both, zero)),
            (FAC, factor),
        ):
            ops_h[t, which], ops_l[t, which] = split(value)

    def make_gain(t):
        inner = product(parts(t, FAC), parts(t, UP), NN)
        turned = split(jnp.transpose(inner))
        gain = -product(turned, parts(t, LOW), NN)
        gains[t, y, :, :HB] = gain[:HB, :HB] + jnp.transpose(gain[HB:, HB:])
        gains[t, y, :, HB:] = gain[HB:, :HB]
        return turned

    def spread_gain(t, i):
        square, corner = gains[t, i, :, :HB], gains[t, i, :, HB:]
        down = lax.broadcasted_iota(jnp.int32, (HB, HB), 0)
        across = lax.broadcasted_iota(jnp.int32, (HB, HB), 1)
        zero = jnp.zeros_like(square)
        first = jnp.where(down > across, square, zero)
        second = jnp.transpose(jnp.where(across > down, square, zero))
        for r, c, value in (
            (0, 0, first),
            (0, 1, zero),
            (1, 0, corner),
            (1, 1, second),
        ):
            high, low = split(value)
            gains_h[t, i, r * HB : (r + 1) * HB, c * HB : (c + 1) * HB] = high
            gains_l[t, i, r * HB : (r + 1) * HB, c * HB : (c + 1) * HB] = low

    def make_shift(t):
        rows = below[t]
        lowered = product(split(rows), parts(t, LOW), NT)
        proj[t] = lowered
        coeffs = split(product(split(lowered), parts(t, FAC), NT))
        d_out[t] = rows - product(coeffs, parts(t, LOW), NN)
        return coeffs

    def make_back(turned, coeffs):
        down = lax.broadcasted_iota(jnp.int32, (NB, NB), 0)
        across = lax.broadcasted_iota(jnp.int32, (NB, NB), 1)
        unit = jnp.where(down == across, 1.0, 0.0).astype(F32)
        back_out[...] = unit - product(turned, parts(0, UP), NN)
        rest_out[...] = -product(coeffs, parts(0, UP), NN)

    def finish(t, rows):
        coeffs = product(split(rows), parts(t, UP), NT) + proj[t]
        coeffs = product(split(coeffs), parts(t, FAC), NT)
        return rows - product(split(coeffs), parts(t, UP), NN)

    def share(column, core):
        at = core * SHARE + column * PART
        return pl.ds(pl.multiple_of(at, PART), PART)

    def half(core):
        return pl.ds(pl.multiple_of(core * SHARE, SHARE), SHARE)

    def source_of(d):
        return (y + NY - d) % NY

    def g_send(t, d):
        piece = gains.at[t, y, share(x, q)]
        return copy(piece, piece, g_s.at[t], g_r.at[t, d - 1], y_peer(d))

    def gx_send(t, d, e):
        piece = gains.at[t, source_of(d), share(x, q)]
        return copy(piece, piece, gx_s.at[t], gx_r.at[t, d - 1], x_peer(e))

    def gq_send(t, d):
        piece = gains.at[t, source_of(d), half(q)]
        return copy(piece, piece, gq_s.at[t], gq_r.at[t, d - 1], sibling)

    def gain_start(t):
        for d in y_near_first:
            g_send(t, d).start()

    def gain_take(t, d):
        arrived(gains.at[t, source_of(d), share(x, q)], g_r.at[t, d - 1])
        for e in near_first:
            gx_send(t, d, e).start()

    def gain_pass(t, d):
        arrived(gains.at[t, 0, pl.ds(0, (NX - 1) * PART)], gx_r.at[t, d - 1])
        gq_send(t, d).start()

    def gain_land(t, d):
        arrived(gains.at[t, source_of(d), half(1 - q)], gq_r.at[t, d - 1])
        spread_gain(t, source_of(d))

    def d_send(t, d):
        there = pl.ds(((y + d) % NY) * CW, CW)
        return copy(
            d_out.at[t, there], d_in.at[t, y], d_s.at[t], d_r.at[t], y_peer(d)
        )

    def send_shift(t):
        for d in y_far_first:
            d_send(t, d).start()
        d_in[t, y] = d_out[t, pl.ds(y * CW, CW)]

    def take_shift(t):
        arrived(d_in.at[t, pl.ds(0, NY - 1)], d_r.at[t])

    def owner_of(t, i):
        return i - 1 if t == 0 else i

    def state_send(t, i):
        return copy(
            states_out.at[t, i],
            states_in.at[t, pl.ds(y * CW, CW)],
            s_s.at[t],
            s_r.at[t],
            (k * NY + owner_of(t, i), col),
        )

    def share_state(t, i):
        if 0 <= owner_of(t, i) < NY:

            @pl.when(y != owner_of(t, i))
            def _():
                state_send(t, i).start()

    def carry_send(t):
        return copy(
            states_out.at[t, NY], carry_in.at[t], c_s.at[t], c_r.at[t], down_group
        )

    middle = has_up & has_down

    def step(t, i, state):
        high, low = split(state)
        pair = dot(jnp.concatenate([high, low], 0), gains_h[t, i], NN)
        return (pair[:CW] + pair[CW:]) + (dot(high, gains_l[t, i], NN) + d_in[t, i])

    def compose(t, with_fresh):
        whole_h[t], whole_l[t] = gains_h[t, 0], gains_l[t, 0]

        def join(i, state):
            longer = product(
                (whole_h[t], whole_l[t]), (gains_h[t, i], gains_l[t, i]), NN
            )
            if with_fresh:
                state = step(t, i, state)
            whole_h[t], whole_l[t] = split(longer)
            return state

        state = lax.fori_loop(1, NY, join, d_in[t, 0])
        if with_fresh:
            fresh[t] = state

    def chain(t):
        if t == 1:
            take_shift(t)

        @pl.when(middle)
        def _():
            if t == 1:
                state = d_in[t, 0]
                for i in range(1, NY):
                    state = step(t, i, state)
                fresh[t] = state
            arrived(carry_in.at[t], c_r.at[t])
            whole = whole_h[t], whole_l[t]
            states_out[t, NY] = product(split(carry_in[t]), whole, NN) + fresh[t]
            carry_send(t).start()
            share_state(t, NY)

        @pl.when((row > 0) & jnp.logical_not(middle))
        def _():
            arrived(carry_in.at[t], c_r.at[t])

        state = carry_in[t]
        for i in range(NY):
            states_out[t, i] = state
            share_state(t, i)
            state = step(t, i, state)

        @pl.when(jnp.logical_not(middle))
        def _():
            states_out[t, NY] = state

            @pl.when(has_down)
            def _():
                carry_send(t).start()

            share_state(t, NY)

    def collect(t):
        mine = pl.ds(y * CW, CW)
        states_in[t, mine] = states_out[t, y + (1 - t)]
        arrived(states_in.at[t, pl.ds(0, (NY - 1) * CW)], s_r.at[t])

    def back_rows(column, core):
        at = (column * NQ + core) * BACK
        return pl.ds(pl.multiple_of(at, BACK), BACK)

    def a_send():
        rows = back_rows(x, q)
        return copy(back_out.at[rows], back_in.at[rows], a_s, a_r, up_row)

    def h_send():
        return copy(rest_out, rest_in, h_s, h_r, up_row)

    def ax_send(d):
        piece = back_in.at[back_rows(x, q)]
        return copy(piece, piece, ax_s, ax_r.at[d - 1], x_peer(d))

    def aq_send(d):
        piece = back_in.at[back_rows((x + NX - d) % NX, q)]
        return copy(piece, piece, aq_s, aq_r, sibling)

    def back_take():
        @pl.when(row < last_row)
        def _():
            arrived(back_in.at[back_rows(x, q)], a_r)
            for d in near_first:
                ax_send(d).start()
            aq_send(0).start()

    def back_pass():
        @pl.when(row < last_row)
        def _():
            for d in near_first:
                arrived(back_in.at[back_rows((x + NX - d) % NX, q)], ax_r.at[d - 1])
                aq_send(d).start()

    def back_land():
        arrived(back_in.at[pl.ds(0, NX * BACK)], aq_r)
        arrived(rest_in, h_r)

    def left(view, sem):
        copy(view, view, sem, z_r.at[0], sibling).wait_send()

    def left_early():
        for t in range(2):
            z_send(t).wait_send()
            left(vf.at[t, pl.ds(0, NX - 1), :, 0], x_s.at[t])
            left(vf.at[t, :, :, 0], q_s.at[t])

        @pl.when(row > 0)
        def _():
            e_send().wait_send()

    def left_ring(t):
        left(gains.at[t, pl.ds(0, NY - 1), pl.ds(0, PART)], g_s.at[t])
        left(gains.at[t, pl.ds(0, NY - 1), pl.ds(0, (NX - 1) * PART)], gx_s.at[t])
        left(gains.at[t, pl.ds(0, NY - 1), pl.ds(0, SHARE)], gq_s.at[t])
        left(d_out.at[t, pl.ds(0, (NY - 1) * CW)], d_s.at[t])

    def left_back():
        @pl.when(row > 0)
        def _():
            a_send().wait_send()
            h_send().wait_send()

        @pl.when(row < last_row)
        def _():
            left(back_in.at[pl.ds(0, (NX - 1) * BACK)], ax_s)
            left(back_in.at[pl.ds(0, NX * BACK)], aq_s)

        @pl.when(row == 0)
        def _():
            for t in range(2):
                left(init.at[t, pl.ds(0, (NY - 1) * CW)], i_s.at[t])

    def left_states(t):
        left(states_out.at[t, pl.ds(0, NY - 1)], s_s.at[t])

        @pl.when(has_down)
        def _():
            carry_send(t).wait_send()

    def each(step, t, ds):
        for d in ds:
            step(t, d)

    near, far = y_near_first[: NY // 2], y_near_first[NY // 2 :]
    unpack(0)
    turned = make_gain(0)
    gain_start(0)
    coeffs = make_shift(0)
    spread_gain(0, y)
    z_take(1)
    each(gain_take, 0, near)
    send_shift(0)
    make_back(turned, coeffs)

    @pl.when(row > 0)
    def _():
        a_send().start()
        h_send().start()

    each(gain_take, 0, far)
    for p in range(2):
        for d in near_first:
            x_take(1, p, d)
    q_take(1)
    unpack(1)
    make_gain(1)
    gain_start(1)
    spread_gain(1, y)
    each(gain_pass, 0, near)
    for d, e in zip(far, near):
        gain_pass(0, d)
        gain_land(0, e)
    for d in y_near_first[len(far) :]:
        gain_land(0, d)
    back_take()

    def bring():
        each(gain_take, 1, y_near_first)

    def hand():
        each(gain_pass, 1, y_near_first)

    def keep():
        each(gain_land, 1, y_near_first)

    @pl.when(k >= 3)
    def _():
        back_pass()

    @pl.when(middle)
    def _():
        take_shift(0)
        compose(0, True)

    @pl.when(k >= 2)
    def _():
        bring()

    @pl.when(jnp.logical_not(middle))
    def _():
        take_shift(0)

    chain(0)

    @pl.when(k < 2)
    def _():
        bring()

    @pl.when(k < 3)
    def _():
        back_pass()

    @pl.when(k >= 2)
    def _():
        hand()

    left_early()
    left_ring(0)
    collect(0)

    @pl.when(row < last_row)
    def _():
        back_land()
        below[1] = rest_in[...] + product(
            split(states_in[0]), split(back_in[...]), NN
        )

    @pl.when(row == last_row)
    def _():
        below[1] = jnp.zeros((CL, NB), F32)

    make_shift(1)
    send_shift(1)

    @pl.when(row == 0)
    def _():
        init[1] = finish(0, init[0])
        send_init(1)

    @pl.when(k < 2)
    def _():
        hand()

    keep()

    @pl.when(middle)
    def _():
        compose(1, False)

    chain(1)
    left_ring(1)
    left_states(0)
    left_back()
    collect(1)
    out_ref[...] = jnp.transpose(finish(1, states_in[1]))
    store = pltpu.make_async_copy(out_ref, out_hbm, own_s.at[3])
    store.start()
    left_states(1)
    store.wait()


def on_device(dims, eigvecs, reflectors, factors, offsets, sweep_order):
    KZ, NY, NX, NH, NQ = dims
    NB, CL = eigvecs.shape
    CW = CL // NY
    RC = reflectors.shape[2]
    DMA = pltpu.SemaphoreType.DMA
    hbm = pl.BlockSpec(memory_space=pltpu.HBM)
    return pl.pallas_call(
        functools.partial(kernel, dims),
        out_shape=jax.ShapeDtypeStruct((NB, CL), F32),
        in_specs=[hbm] * 5,
        out_specs=pl.BlockSpec(memory_space=pl.ANY),
        scratch_shapes=[
            pltpu.SMEM(sweep_order.shape, jnp.int32),
            pltpu.SMEM((offsets.shape[0],), jnp.int32),
            pltpu.VMEM(eigvecs.shape, F32),
            pltpu.VMEM(reflectors.shape, F32),
            pltpu.VMEM(factors.shape, F32),
            pltpu.VMEM(eigvecs.shape, F32),
            DMA((6,)),
            pltpu.VMEM((2, NX, NH, NQ, 2 * RC, NB), F32),
            pltpu.VMEM((2, 3, NB, NB), BF16),
            pltpu.VMEM((2, 3, NB, NB), BF16),
            pltpu.VMEM((2, CL, NB), F32),
            pltpu.VMEM((NB, CL), F32),
            pltpu.VMEM((2, CL, NB), F32),
            pltpu.VMEM((2, CL, NB), F32),
            pltpu.VMEM((2, NY, NB // 2, NB), F32),
            pltpu.VMEM((2, NY, NB, NB), BF16),
            pltpu.VMEM((2, NY, NB, NB), BF16),
            pltpu.VMEM((2, CL, NB), F32),
            pltpu.VMEM((2, NY, CW, NB), F32),
            pltpu.VMEM((2, CW, NB), F32),
            pltpu.VMEM((2, NY + 1, CW, NB), F32),
            pltpu.VMEM((2, CL, NB), F32),
            pltpu.VMEM((2, NB, NB), BF16),
            pltpu.VMEM((2, NB, NB), BF16),
            pltpu.VMEM((2, CW, NB), F32),
            pltpu.VMEM((NB, NB), F32),
            pltpu.VMEM((NB, NB), F32),
            pltpu.VMEM((CL, NB), F32),
            pltpu.VMEM((CL, NB), F32),
            DMA((2,)),
            DMA((2,)),
            DMA((2,)),
            DMA((2, NH, NX)),
            DMA((2,)),
            DMA((2,)),
            DMA,
            DMA,
            DMA((2,)),
            DMA((2, NY - 1)),
            DMA((2,)),
            DMA((2, NY - 1)),
            DMA((2,)),
            DMA((2, NY - 1)),
            DMA((2,)),
            DMA((2,)),
            DMA((2,)),
            DMA((2,)),
            DMA((2,)),
            DMA((2,)),
            DMA((2,)),
            DMA,
            DMA,
            DMA,
            DMA,
            DMA,
            DMA((NX - 1,)),
            DMA,
            DMA,
        ],
        compiler_params=pltpu.CompilerParams(
            collective_id=0, has_side_effects=True, vmem_limit_bytes=24 << 20
        ),
    )(
        *(
            pltpu.with_memory_space_constraint(part, pltpu.HBM)
            for part in (
                sweep_order,
                offsets.reshape(-1),
                eigvecs,
                reflectors,
                factors,
            )
        ),
    )


def build(mesh, dims):
    placed = (
        P("row", "col"),
        P(None, "row", "col", None),
        P(None, "row", "col", None),
        P(None, "row"),
        P(),
    )
    return jax.shard_map(
        functools.partial(on_device, dims),
        mesh=mesh,
        in_specs=placed,
        out_specs=P("row", "col"),
        check_vma=False,
    )


def solution(mesh):
    return build(mesh, (Z_LO, Y, X, Z_HI, CORES))
```
